32 devices in a mesh: groups: 2 (over y), seq: 4 (over z), chan: 2 (over x), sub: 2 (over core).
Axes of the slice: x: 2, y: 2, z: 4, core: 2. Of those that a mesh axis runs over, the one named last changes fastest.
Arguments:
- x_in: bfloat16 [1024, 8192], P(('groups', 'seq'), ('chan', 'sub')), parts along dimension 0, may hold values from -36 to 36
- b_in: bfloat16 [1024, 4, 256], P(('groups', 'seq'), 'chan'), parts along dimension 0, may hold values from -6 to 6
- c_in: bfloat16 [1024, 4, 256], P(('groups', 'seq'), 'chan'), parts along dimension 0, may hold values from -0.375 to 0.375
- step_size: float32 [1024, 128], P(('groups', 'seq'), ('chan', 'sub')), parts along dimension 0, may hold values from 0.02 to 0.2
- log_decay: float32 [1024, 128], P(('groups', 'seq'), ('chan', 'sub')), parts along dimension 0, may hold values from -1 to 0, as said below
- skip: float32 [128], P(('chan', 'sub')), may hold values from 0.5 to 1.5
- gate_in: bfloat16 [1024, 8192], P(('groups', 'seq'), ('chan', 'sub')), parts along dimension 0, may hold values from -6 to 6
- norm_gain: float32 [8192], P(('chan', 'sub')), may hold values from 0.1 to 1.9
- walsh_sign: int32 [8192], P(('chan', 'sub')), may hold values from 0 to 1
- channel_shift_power: int32 [8192], P(('chan', 'sub')), may hold values from -1 to 3
- out_weight: bfloat16 [8192, 4096], P(('chan', 'sub'), 'seq'), may hold values from -0.0625 to 0.0625
Outputs:
- projected: bfloat16 [1024, 4096], P(('groups', 'seq', 'chan', 'sub')), parts along dimension 0
The draws below stay inside these ranges and needn't reach their ends.
There are 2 independent parts, one for each index of `groups`. The reference program is written for one: setup_inputs(seed, part) draws one part's arguments, and reference() takes and returns one part's arrays. A program takes and returns all parts, laid end to end along the dimension named above; an argument that names none is the same for every part. Nothing has to cross between parts.
Inputs may be any that keep to these rules, and one draw needn't show every extreme that they name: `log_decay`: every entry is negative.
All inputs are finite; a program needn't handle non-finite values.
Results may differ from the reference program's by a relative error of at most 0.024.
Values may be sent and summed in bfloat16 or wider, within the bound.
A program may use at most 128 MiB of HBM per device.

```python
import math
import jax
import jax.numpy as jnp
from jax import lax

LOCAL_HEADS = 128
P_SIZE = 64
N = 256
G = 4
NORM_HEADS = 16
OUT = 4096
TOK_DEV = 128
CONTEXT_TOKENS = 512
N_CHAN = 2
N_SUB = 2


def draw_x_in(key, part):
    key_head, key_body = jax.random.split(key, 2)
    head_ids = jnp.arange(LOCAL_HEADS)
    rising = 3.0 ** ((head_ids % (LOCAL_HEADS // G)).astype(jnp.float32) / max(LOCAL_HEADS // G - 1, 1))
    spread = jnp.exp(jax.random.uniform(key_head, (LOCAL_HEADS,), jnp.float32, 0.0, math.log(3.0)))
    head_scale = jnp.repeat(rising * spread, P_SIZE)
    values = jnp.clip(jax.random.normal(key_body, (CONTEXT_TOKENS, LOCAL_HEADS * P_SIZE), jnp.float32), -4.0, 4.0)
    return (values * head_scale[None, :]).astype(jnp.bfloat16)


def draw_log_decay(key, part):
    random_subkey_list = jax.random.split(key, 7)
    slow_share = 0.5
    is_slow = jax.random.bernoulli(random_subkey_list[0], slow_share, (LOCAL_HEADS,))
    slow_rate = jnp.exp(jax.random.uniform(random_subkey_list[1], (LOCAL_HEADS,), jnp.float32, math.log(0.1), math.log(0.5))) / CONTEXT_TOKENS
    fast_rate = jnp.exp(jax.random.uniform(random_subkey_list[2], (LOCAL_HEADS,), jnp.float32, math.log(1.0 / 50.0), math.log(1.0 / 30.0)))
    head_decay_speed = jnp.where(is_slow, slow_rate, fast_rate)
    block_multiplier = jnp.repeat(jnp.exp(jax.random.uniform(random_subkey_list[3], (CONTEXT_TOKENS // TOK_DEV,), jnp.float32, math.log(0.5), math.log(2.0))), TOK_DEV)
    element_multiplier = jnp.exp(jax.random.uniform(random_subkey_list[4], (CONTEXT_TOKENS, LOCAL_HEADS), jnp.float32, math.log(0.5), math.log(2.0)))
    outlier_token_index = jax.random.randint(random_subkey_list[5], (2,), 0, CONTEXT_TOKENS)
    outlier_cost_factor = jax.random.uniform(random_subkey_list[6], (2, LOCAL_HEADS), jnp.float32, 0.2, 0.4)
    outlier_found = (jnp.arange(CONTEXT_TOKENS)[:, None] == outlier_token_index[None, :]).astype(jnp.float32)
    outlier_feature = jnp.sum(outlier_found[:, :, None] * jnp.log(1.0 - outlier_cost_factor)[None, :, :], axis=1)
    return (-head_decay_speed[None, :] * block_multiplier[:, None] * element_multiplier + outlier_feature).astype(jnp.float32)


def with_ends(values, stream_key, least, high):
    dims = values.shape
    place = [jax.random.randint(jax.random.fold_in(stream_key, axis), (), 0, dims[axis]) for axis in range(len(dims))]
    values = values.at[tuple(place)].set(least)
    longest = dims.index(max(dims))
    place[longest] = (place[longest] + 1) % dims[longest]
    return values.at[tuple(place)].set(high)


def level_of(stream_key, shape, shards, smallest, top_value):
    level, own = 1.0, jax.random.fold_in(stream_key, 6)
    for axis_at, parts in shards:
        heights = jnp.exp(jax.random.uniform(jax.random.fold_in(own, axis_at), (parts,), jnp.float32, smallest / len(shards), top_value / len(shards)))
        level = level * jnp.repeat(heights, shape[axis_at] // parts).reshape([-1 if axis == axis_at else 1 for axis in range(len(shape))])
    return level


def noise(own_key, extent, deviation, limit, cuts=(), kind=jnp.bfloat16):
    values = deviation * jax.random.normal(own_key, extent, jnp.float32)
    if cuts:
        values = values * level_of(own_key, extent, cuts, -0.22, 0.18)
    return jnp.clip(values, -limit, limit).astype(kind)


def setup_inputs(seed: int = 0, part: int = 0) -> dict:
    splits = jax.random.split(jax.random.key(seed), 12)
    own_keys = jax.random.split(jax.random.fold_in(splits[11], part), 12)
    return {
        "x_in": draw_x_in(jax.random.fold_in(jax.random.fold_in(splits[11], part), 71), part),
        "b_in": noise(own_keys[1], (CONTEXT_TOKENS, G, N), 1.0, 6.0, ((0, 4), (1, 2))),
        "c_in": noise(own_keys[2], (CONTEXT_TOKENS, G, N), N ** -0.5, 0.375, ((0, 4), (1, 2))),
        "step_size": jnp.clip(jnp.exp(math.log(0.2) - 2.3025851 * jax.random.uniform(own_keys[3], (CONTEXT_TOKENS, LOCAL_HEADS), jnp.float32) ** level_of(own_keys[3], (CONTEXT_TOKENS, LOCAL_HEADS), ((0, 4), (1, 4)), -0.2, 0.2)), 0.02, 0.2),
        "log_decay": draw_log_decay(jax.random.fold_in(jax.random.fold_in(splits[11], part), 71), part),
        "skip": jnp.clip(0.5 + 1.0 * jax.random.uniform(splits[5], (LOCAL_HEADS,), jnp.float32) ** level_of(splits[5], (LOCAL_HEADS,), ((0, 4),), -0.2, 0.2), 0.5, 1.5),
        "gate_in": noise(own_keys[6], (CONTEXT_TOKENS, LOCAL_HEADS * P_SIZE), 1.0, 6.0, ((0, 4), (1, 4))),
        "norm_gain": jnp.clip(1.0 + 0.18 * jax.random.normal(splits[7], (LOCAL_HEADS * P_SIZE,), jnp.float32), 0.1, 1.9),
        "walsh_sign": with_ends(jax.random.randint(splits[8], (LOCAL_HEADS * P_SIZE,), 0, 2), jax.random.fold_in(splits[8], 1), 0, 1).astype(jnp.int32),
        "channel_shift_power": with_ends(jax.random.randint(splits[9], (LOCAL_HEADS * P_SIZE,), -1, 4), jax.random.fold_in(splits[9], 1), -1, 3).astype(jnp.int32),
        "out_weight": noise(splits[10], (LOCAL_HEADS * P_SIZE, OUT), (LOCAL_HEADS * P_SIZE) ** -0.5, 0.0625, ((0, 4), (1, 4))),
    }


norm_eps = 1e-05
clip_level = 4.0
expo_levels = (-1, 0, 1, 2, 3)

def power_two(expo, sign_flip):
    result = jnp.zeros(expo.shape, jnp.float32)
    for level in expo_levels:
        result = result + jnp.where(expo == level, jnp.float32(2.0 ** (sign_flip * level)), jnp.float32(0.0))
    return result

def walsh_rows(values):
    row_count, width = values.shape
    half_span = 1
    while half_span < width:
        shaped = values.reshape(row_count, width // (2 * half_span), 2, half_span)
        upper = shaped[:, :, 0, :]
        lower = shaped[:, :, 1, :]
        values = jnp.stack([upper + lower, upper - lower], axis=2).reshape(row_count, width)
        half_span = half_span * 2
    return values

def reference(x_in, b_in, c_in, step_size, log_decay, skip, gate_in, norm_gain, walsh_sign, channel_shift_power, out_weight):
    highest = lax.Precision.HIGHEST
    head_group = LOCAL_HEADS // G
    block_len = math.gcd(CONTEXT_TOKENS, 256)
    block_count = CONTEXT_TOKENS // block_len
    x_heads = x_in.astype(jnp.float32).reshape(CONTEXT_TOKENS, LOCAL_HEADS, P_SIZE)
    weighted = x_heads * step_size[:, :, None]

    def one_block(state, block_index):
        start = (block_index * block_len).astype(jnp.int32)
        x_block = lax.dynamic_slice_in_dim(weighted, start, block_len, 0).reshape(block_len, G, head_group, P_SIZE)
        b_block = lax.dynamic_slice_in_dim(b_in, start, block_len, 0).astype(jnp.float32)
        c_block = lax.dynamic_slice_in_dim(c_in, start, block_len, 0).astype(jnp.float32)
        decay_block = lax.dynamic_slice_in_dim(log_decay, start, block_len, 0)
        cumul = jnp.cumsum(decay_block, axis=0)
        inner = jnp.einsum('tgn,ugn->tug', c_block, b_block, precision=highest)
        differ = cumul[:, None, :] - cumul[None, :, :]
        causal = (jnp.arange(block_len)[:, None] >= jnp.arange(block_len)[None, :])[:, :, None]
        ratio = jnp.where(causal, jnp.exp(jnp.where(causal, differ, 0.0)), 0.0).reshape(block_len, block_len, G, head_group)
        mixing = ratio * inner[:, :, :, None]
        y_diag = jnp.einsum('tugk,ugkp->tgkp', mixing, x_block, precision=highest)
        y_off = jnp.einsum('tgn,gnkp->tgkp', c_block, state, precision=highest) * jnp.exp(cumul).reshape(block_len, G, head_group)[:, :, :, None]
        total = cumul[-1]
        to_end = jnp.exp(total[None, :] - cumul).reshape(block_len, G, head_group)[:, :, :, None]
        new_state = state * jnp.exp(total).reshape(G, 1, head_group, 1) + jnp.einsum('ugn,ugkp->gnkp', b_block, x_block * to_end, precision=highest)
        return (new_state, (y_diag + y_off).reshape(block_len, LOCAL_HEADS * P_SIZE))
    initial = jnp.zeros((G, N, head_group, P_SIZE), jnp.float32)
    final_state, y_blocks = lax.scan(one_block, initial, jnp.arange(block_count, dtype=jnp.int32))
    y_ssm = y_blocks.reshape(CONTEXT_TOKENS, LOCAL_HEADS * P_SIZE) + (x_heads * skip[None, :, None]).reshape(CONTEXT_TOKENS, LOCAL_HEADS * P_SIZE)
    gated_pre = y_ssm * jax.nn.silu(gate_in.astype(jnp.float32))
    grouped = gated_pre.reshape(CONTEXT_TOKENS, LOCAL_HEADS // NORM_HEADS, NORM_HEADS * P_SIZE)
    mean_sq = lax.optimization_barrier(jnp.mean(grouped * grouped, axis=2, keepdims=True))
    gated = (grouped * lax.rsqrt(mean_sq + norm_eps)).reshape(CONTEXT_TOKENS, LOCAL_HEADS * P_SIZE) * norm_gain[None, :]
    gated = gated.astype(jnp.bfloat16)
    sign_value = jnp.where(walsh_sign == 1, 1.0, -1.0).astype(jnp.float32)
    signed = gated.astype(jnp.float32) * sign_value[None, :]
    rotated = walsh_rows(signed) * (1.0 / math.sqrt(LOCAL_HEADS * P_SIZE))
    quant = jnp.clip(rotated * power_two(channel_shift_power, 1)[None, :], -clip_level, clip_level).astype(jnp.bfloat16)
    scaled = (lax.optimization_barrier(quant).astype(jnp.float32) * power_two(channel_shift_power, -1)[None, :]).astype(jnp.bfloat16)
    slab_count = N_CHAN * N_SUB
    slab_width = LOCAL_HEADS * P_SIZE // slab_count

    def add_slab(slab_index, accum):
        offset = (slab_index * slab_width).astype(jnp.int32)
        columns = lax.dynamic_slice_in_dim(scaled, offset, slab_width, 1)
        weight_rows = lax.dynamic_slice_in_dim(out_weight, offset, slab_width, 0)
        slab_partial = jnp.dot(columns, weight_rows, preferred_element_type=jnp.float32).astype(jnp.bfloat16)
        return accum + lax.optimization_barrier(slab_partial).astype(jnp.float32)
    summed = lax.fori_loop(jnp.int32(0), jnp.int32(slab_count), add_slab, jnp.zeros((CONTEXT_TOKENS, OUT), jnp.float32))
    return summed.astype(jnp.bfloat16)
```

```python
import functools
import math

import jax
import jax.numpy as jnp
from jax import lax
from jax.experimental import pallas as pl
from jax.experimental.pallas import tpu as pltpu
from jax.sharding import PartitionSpec as P

LOCAL_HEADS = 128
P_SIZE = 64
G = 4
NORM_HEADS = 16


norm_eps = 1e-05
clip_level = 4.0
expo_levels = (-1, 0, 1, 2, 3)
lanes = 128
MESH = pl.DeviceIdType.MESH


def partner_2(block, axis, bit):
    count = lax.axis_size(axis)
    route = []
    for low in range(count):
        high = low | 1 << bit
        if high != low and high < count:
            route += [(low, high), (high, low)]
    return lax.ppermute(block, axis, route)


def power_two(expo, sign_flip):
    result = jnp.zeros(expo.shape, jnp.float32)
    for level in expo_levels:
        result = result + jnp.where(
            expo == level, jnp.float32(2.0 ** (sign_flip * level)), jnp.float32(0.0)
        )
    return result


def sylvester(order):
    indices = jnp.arange(order, dtype=jnp.int32)
    oddness_flag = jnp.zeros((order, order), jnp.int32)
    for bit_index in range(order.bit_length() - 1):
        stride = 2**bit_index
        oddness_flag = oddness_flag + indices[:, None] // stride % 2 * (
            indices[None, :] // stride % 2
        )
    return (1 - 2 * (oddness_flag % 2)).astype(jnp.bfloat16)


def halves(value):
    upper = value.astype(jnp.bfloat16)
    return upper, (value - upper.astype(jnp.float32)).astype(jnp.bfloat16)


def dot32(left, right):
    return jnp.dot(left, right, preferred_element_type=jnp.float32)


def earlier_kernel(
    n, tile, x_ref, b_ref, total_ref, c_ref, y_ref, x_in, b_in, total_in, run, send, recv
):
    me = lax.axis_index("seq")
    barrier = pltpu.get_barrier_semaphore()

    @pl.loop(1, n)
    def _(d):
        pl.semaphore_signal(
            barrier, inc=1, device_id={"seq": lax.rem(me + d, n)}, device_id_type=MESH
        )

    pl.semaphore_wait(barrier, n - 1)

    def copies(d):
        target = {"seq": lax.rem(me + d, n)}
        pairs = ((b_ref, b_in), (total_ref, total_in), (x_ref, x_in))
        return [
            pltpu.make_async_remote_copy(
                src_ref=source,
                dst_ref=landing.at[d],
                send_sem=send.at[d, i],
                recv_sem=recv.at[d, i],
                device_id=target,
                device_id_type=MESH,
            )
            for i, (source, landing) in enumerate(pairs)
        ]

    @pl.loop(1, n)
    def _(d):
        @pl.when(me + d < n)
        def _():
            for copy in copies(d):
                copy.start()

    y_ref[...] = jnp.zeros_like(y_ref)
    run[...] = jnp.zeros_like(run)

    @pl.loop(1, n)
    def _(d):
        @pl.when(me >= d)
        def _():
            for copy in copies(d):
                copy.wait_recv()
            mixing = lax.dot_general(
                c_ref[...],
                b_in[d],
                (((1,), (1,)), ((), ())),
                preferred_element_type=jnp.float32,
            )
            upper, lower = halves(mixing)

            @pl.loop(0, y_ref.shape[1] // tile)
            def _(i):
                at = pl.ds(pl.multiple_of(i * tile, tile), tile)
                block = x_in[d, :, at]
                y_ref[:, at] += (dot32(upper, block) + dot32(lower, block)) * jnp.exp(run[:, at])

            run[...] += total_in[d]

    @pl.loop(1, n)
    def _(d):
        @pl.when(me + d < n)
        def _():
            for copy in copies(d):
                copy.wait_send()


def earlier_blocks(x_end, b_group, total, c_group):
    n = lax.axis_size("seq")
    rows, width = x_end.shape
    vmem = pl.BlockSpec(memory_space=pltpu.VMEM)
    return pl.pallas_call(
        functools.partial(earlier_kernel, n, min(512, width)),
        out_shape=jax.ShapeDtypeStruct((rows, width), jnp.float32),
        in_specs=[vmem] * 4,
        out_specs=vmem,
        scratch_shapes=[
            pltpu.VMEM((n, rows, width), jnp.bfloat16),
            pltpu.VMEM((n, rows, b_group.shape[1]), jnp.bfloat16),
            pltpu.VMEM((n, 1, width), jnp.float32),
            pltpu.VMEM((1, width), jnp.float32),
            pltpu.SemaphoreType.DMA((n, 3)),
            pltpu.SemaphoreType.DMA((n, 3)),
        ],
        compiler_params=pltpu.CompilerParams(
            collective_id=0, has_side_effects=True, vmem_limit_bytes=48 * 2**20
        ),
    )(x_end, b_group, total, c_group)


def rotate_kernel(factor, mixed_ref, table_ref, up_ref, down_ref, out_ref):
    count = mixed_ref.shape[1] // lanes
    parts = [mixed_ref[:, i * lanes : (i + 1) * lanes] for i in range(count)]
    span = 1
    while span < count:
        for i in range(count):
            if not i & span:
                a, b = parts[i], parts[i + span]
                parts[i], parts[i + span] = a + b, a - b
        span *= 2
    table = table_ref[...]
    for i in range(count):
        at = slice(i * lanes, (i + 1) * lanes)
        upper, lower = halves(parts[i])
        rotated = (dot32(upper, table) + dot32(lower, table)) * factor
        quant = jnp.clip(rotated * up_ref[:, at], -clip_level, clip_level).astype(jnp.bfloat16)
        out_ref[:, at] = (quant.astype(jnp.float32) * down_ref[:, at]).astype(jnp.bfloat16)


def rotate(mixed, up, down):
    vmem = pl.BlockSpec(memory_space=pltpu.VMEM)
    return pl.pallas_call(
        functools.partial(rotate_kernel, 1.0 / math.sqrt(LOCAL_HEADS * P_SIZE)),
        out_shape=jax.ShapeDtypeStruct(mixed.shape, jnp.bfloat16),
        in_specs=[vmem] * 4,
        out_specs=vmem,
    )(mixed, sylvester(lanes), up[None, :], down[None, :])


def project_kernel(
    n,
    n_chan,
    n_sub,
    tile,
    scaled_ref,
    weight_hbm,
    out_ref,
    weight,
    slots,
    partial,
    slabs,
    summed,
    landed,
    local_sem,
    g_send,
    g_recv,
    s_send,
    s_recv,
    f_send,
    f_recv,
):
    me = lax.axis_index("seq")
    peers = n_chan * n_sub
    here = lax.axis_index("chan") * n_sub + lax.axis_index("sub")
    rows, feats = out_ref.shape[0], weight.shape[1]

    def slab_device(e):
        other = lax.rem(here + e, peers)
        return other, {"chan": other // n_sub, "sub": lax.rem(other, n_sub)}

    fetch = pltpu.make_async_copy(weight_hbm, weight, local_sem.at[0])
    own = pltpu.make_async_copy(scaled_ref, slots.at[0], local_sem.at[1])
    fetch.start()
    own.start()
    barrier = pltpu.get_barrier_semaphore()

    @pl.loop(1, n)
    def _(d):
        pl.semaphore_signal(
            barrier, inc=1, device_id={"seq": lax.rem(me + d, n)}, device_id_type=MESH
        )

    @pl.loop(1, peers)
    def _(e):
        pl.semaphore_signal(barrier, inc=1, device_id=slab_device(e)[1], device_id_type=MESH)

    pl.semaphore_wait(barrier, n - 1 + peers - 1)

    def offset(s):
        return jnp.where(lax.rem(s, 2) == 1, (s + 1) // 2, lax.rem(n - s // 2, n))

    def gather(d):
        return pltpu.make_async_remote_copy(
            src_ref=scaled_ref,
            dst_ref=slots.at[d],
            send_sem=g_send.at[d],
            recv_sem=g_recv.at[d],
            device_id={"seq": lax.rem(me + d, n)},
            device_id_type=MESH,
        )

    def slab(d, e):
        other, device = slab_device(e)
        return pltpu.make_async_remote_copy(
            src_ref=partial.at[d, pl.ds(pl.multiple_of(other * rows, rows), rows)],
            dst_ref=slabs.at[d, e],
            send_sem=s_send.at[d, e],
            recv_sem=s_recv.at[d, e],
            device_id=device,
            device_id_type=MESH,
        )

    def finish(d):
        return pltpu.make_async_remote_copy(
            src_ref=summed.at[d],
            dst_ref=landed.at[d],
            send_sem=f_send.at[d],
            recv_sem=f_recv.at[d],
            device_id={"seq": lax.rem(me - d + n, n)},
            device_id_type=MESH,
        )

    @pl.loop(1, n)
    def _(s):
        gather(offset(s)).start()

    own.wait()
    fetch.wait()

    def reduce_block(s):
        d = offset(s)

        @pl.loop(1, peers)
        def _(e):
            slab(d, e).wait_recv()

        mine = pl.ds(pl.multiple_of(here * rows, rows), rows)
        total = partial[d, mine, :].astype(jnp.float32)
        for e in range(1, peers):
            total = total + slabs[d, e].astype(jnp.float32)
        summed[d] = total.astype(jnp.bfloat16)

        @pl.when(d > 0)
        def _():
            finish(d).start()

    @pl.loop(0, n)
    def _(s):
        d = offset(s)

        @pl.when(s > 0)
        def _():
            gather(d).wait_recv()

        @pl.loop(0, feats // tile)
        def _(i):
            at = pl.ds(pl.multiple_of(i * tile, tile), tile)
            partial[d, :, at] = dot32(slots[d], weight[:, at]).astype(jnp.bfloat16)

        @pl.loop(1, peers)
        def _(e):
            slab(d, e).start()

        @pl.when(s > 0)
        def _():
            reduce_block(s - 1)

    reduce_block(n - 1)

    def columns(d):
        return pl.ds(pl.multiple_of(lax.rem(me + d, n) * feats, feats), feats)

    out_ref[:, columns(0)] = summed[0]

    @pl.loop(1, n)
    def _(s):
        d = offset(s)
        finish(d).wait_recv()
        out_ref[:, columns(d)] = landed[d]

    @pl.loop(1, n)
    def _(d):
        gather(d).wait_send()
        finish(d).wait_send()

    @pl.loop(0, n)
    def _(d):
        @pl.loop(1, peers)
        def _(e):
            slab(d, e).wait_send()


def project(scaled, weight):
    n, n_chan, n_sub = (lax.axis_size(axis) for axis in ("seq", "chan", "sub"))
    peers = n_chan * n_sub
    rows, depth = scaled.shape
    feats = weight.shape[1]
    own_rows = rows // peers
    vmem = pl.BlockSpec(memory_space=pltpu.VMEM)
    dma = pltpu.SemaphoreType.DMA
    return pl.pallas_call(
        functools.partial(project_kernel, n, n_chan, n_sub, min(256, feats)),
        out_shape=jax.ShapeDtypeStruct((own_rows, n * feats), jnp.bfloat16),
        in_specs=[vmem, pl.BlockSpec(memory_space=pl.ANY)],
        out_specs=vmem,
        scratch_shapes=[
            pltpu.VMEM(weight.shape, jnp.bfloat16),
            pltpu.VMEM((n, rows, depth), jnp.bfloat16),
            pltpu.VMEM((n, rows, feats), jnp.bfloat16),
            pltpu.VMEM((n, peers, own_rows, feats), jnp.bfloat16),
            pltpu.VMEM((n, own_rows, feats), jnp.bfloat16),
            pltpu.VMEM((n, own_rows, feats), jnp.bfloat16),
            dma((2,)),
            dma((n,)),
            dma((n,)),
            dma((n, peers)),
            dma((n, peers)),
            dma((n,)),
            dma((n,)),
        ],
        compiler_params=pltpu.CompilerParams(
            collective_id=1, has_side_effects=True, vmem_limit_bytes=48 * 2**20
        ),
    )(scaled, weight)


def body(
    x_in,
    b_in,
    c_in,
    step_size,
    log_decay,
    skip,
    gate_in,
    norm_gain,
    walsh_sign,
    channel_shift_power,
    out_weight,
):
    highest = lax.Precision.HIGHEST
    tok_rows, chan_width = x_in.shape
    head_local = step_size.shape[1]
    head_group = LOCAL_HEADS // G
    sub_index = lax.axis_index("sub")
    group_local = sub_index * head_local // head_group
    b_group = lax.dynamic_slice_in_dim(b_in, group_local, 1, 1)[:, 0, :]
    c_group = lax.dynamic_slice_in_dim(c_in, group_local, 1, 1)[:, 0, :]
    x_heads = x_in.astype(jnp.float32).reshape(tok_rows, head_local, P_SIZE)
    weighted = x_heads * step_size[:, :, None]
    cumul = jnp.cumsum(log_decay, axis=0)
    inner = jnp.dot(c_group, b_group.T, preferred_element_type=jnp.float32)
    differ = cumul[:, None, :] - cumul[None, :, :]
    causal = (jnp.arange(tok_rows)[:, None] >= jnp.arange(tok_rows)[None, :])[:, :, None]
    ratio = jnp.where(causal, jnp.exp(jnp.where(causal, differ, 0.0)), 0.0)
    mixing = ratio * inner[:, :, None]
    y_diag = jnp.einsum("tuh,uhp->thp", mixing, weighted, precision=highest).reshape(
        tok_rows, chan_width
    )
    to_end = jnp.exp(cumul[-1][None, :] - cumul)
    x_end = (weighted * to_end[:, :, None]).reshape(tok_rows, chan_width).astype(jnp.bfloat16)
    total = jnp.repeat(cumul[-1], P_SIZE)[None, :]
    y_off = earlier_blocks(x_end, b_group, total, c_group) * jnp.repeat(
        jnp.exp(cumul), P_SIZE, axis=1
    )
    y_ssm = y_diag + y_off + (x_heads * skip[None, :, None]).reshape(tok_rows, chan_width)
    gated_pre = y_ssm * jax.nn.silu(gate_in.astype(jnp.float32))
    grouped = gated_pre.reshape(tok_rows, head_local // NORM_HEADS, NORM_HEADS * P_SIZE)
    mean_sq = jnp.mean(grouped * grouped, axis=2, keepdims=True)
    gated = (
        (grouped * lax.rsqrt(mean_sq + norm_eps)).reshape(tok_rows, chan_width) * norm_gain[None, :]
    ).astype(jnp.bfloat16)
    sign_value = jnp.where(walsh_sign == 1, 1.0, -1.0).astype(jnp.bfloat16)
    signed = gated * sign_value[None, :]
    partner = partner_2(signed, "sub", 0)
    own_float = signed.astype(jnp.float32)
    partner_float = partner.astype(jnp.float32)
    mixed = jnp.where(sub_index % 2 == 1, partner_float - own_float, own_float + partner_float)
    chan_index = lax.axis_index("chan")
    for bit_index in range(lax.axis_size("chan").bit_length() - 1):
        partner = partner_2(mixed.astype(jnp.bfloat16), "chan", bit_index).astype(mixed.dtype)
        chan_bit = chan_index // 2**bit_index % 2
        mixed = jnp.where(chan_bit == 1, partner - mixed, mixed + partner)
    scaled = rotate(mixed, power_two(channel_shift_power, 1), power_two(channel_shift_power, -1))
    return project(scaled, out_weight)


def solution(mesh):
    return jax.shard_map(
        body,
        mesh=mesh,
        in_specs=(
            P(("groups", "seq"), ("chan", "sub")),
            P(("groups", "seq"), "chan", None),
            P(("groups", "seq"), "chan", None),
            P(("groups", "seq"), ("chan", "sub")),
            P(("groups", "seq"), ("chan", "sub")),
            P(("chan", "sub")),
            P(("groups", "seq"), ("chan", "sub")),
            P(("chan", "sub")),
            P(("chan", "sub")),
            P(("chan", "sub")),
            P(("chan", "sub"), "seq"),
        ),
        out_specs=P(("groups", "seq", "chan", "sub"), None),
        check_vma=False,
    )
```

```python
import functools
import math

import jax
import jax.numpy as jnp
from jax import lax
from jax.experimental import pallas as pl
from jax.experimental.pallas import tpu as pltpu
from jax.sharding import PartitionSpec as P

LOCAL_HEADS = 128
P_SIZE = 64
G = 4
NORM_HEADS = 16


norm_eps = 1e-05
clip_level = 4.0
expo_levels = (-1, 0, 1, 2, 3)
lanes = 128
MESH = pl.DeviceIdType.MESH


def partner_2(block, axis, bit):
    count = lax.axis_size(axis)
    route = []
    for low in range(count):
        high = low | 1 << bit
        if high != low and high < count:
            route += [(low, high), (high, low)]
    return lax.ppermute(block, axis, route)


def power_two(expo, sign_flip):
    result = jnp.zeros(expo.shape, jnp.float32)
    for level in expo_levels:
        result = result + jnp.where(
            expo == level, jnp.float32(2.0 ** (sign_flip * level)), jnp.float32(0.0)
        )
    return result


def sylvester(order):
    indices = jnp.arange(order, dtype=jnp.int32)
    oddness_flag = jnp.zeros((order, order), jnp.int32)
    for bit_index in range(order.bit_length() - 1):
        stride = 2**bit_index
        oddness_flag = oddness_flag + indices[:, None] // stride % 2 * (
            indices[None, :] // stride % 2
        )
    return (1 - 2 * (oddness_flag % 2)).astype(jnp.bfloat16)


def halves(value):
    upper = value.astype(jnp.bfloat16)
    return upper, (value - upper.astype(jnp.float32)).astype(jnp.bfloat16)


def dot32(left, right):
    return jnp.dot(left, right, preferred_element_type=jnp.float32)


def carry_kernel(
    n, tile, x_ref, bt_ref, total_ref, c_ref, y_ref, arrived, leaving, send, recv
):
    me = lax.axis_index("seq")
    right, left = lax.rem(me + 1, n), lax.rem(me + n - 1, n)
    barrier = pltpu.get_barrier_semaphore()
    for near in (left, right):
        pl.semaphore_signal(barrier, inc=1, device_id={"seq": near}, device_id_type=MESH)
    pl.semaphore_wait(barrier, 2)

    def copy(i):
        return pltpu.make_async_remote_copy(
            src_ref=leaving.at[i],
            dst_ref=arrived.at[i],
            send_sem=send.at[i],
            recv_sem=recv.at[i],
            device_id={"seq": right},
            device_id_type=MESH,
        )

    @pl.loop(0, y_ref.shape[1] // tile)
    def _(i):
        at = pl.ds(pl.multiple_of(i * tile, tile), tile)
        upper, lower = halves(x_ref[:, at])
        own = dot32(bt_ref[...], upper) + dot32(bt_ref[...], lower)

        @pl.when(me == 0)
        def _():
            leaving[i] = own.astype(jnp.bfloat16)
            y_ref[:, at] = jnp.zeros((y_ref.shape[0], tile), jnp.float32)

        @pl.when(me > 0)
        def _():
            copy(i).wait_recv()
            state = arrived[i]
            leaving[i] = (state.astype(jnp.float32) * jnp.exp(total_ref[:, at]) + own).astype(
                jnp.bfloat16
            )

        @pl.when(me + 1 < n)
        def _():
            copy(i).start()

        @pl.when(me > 0)
        def _():
            y_ref[:, at] = dot32(c_ref[...], arrived[i])

    @pl.when(me + 1 < n)
    def _():
        @pl.loop(0, y_ref.shape[1] // tile)
        def _(i):
            copy(i).wait_send()


def carry(x_end, b_group, total, c_group):
    n = lax.axis_size("seq")
    rows, width = x_end.shape
    tile = min(256, width)
    tiles = width // tile
    states = b_group.shape[1]
    vmem = pl.BlockSpec(memory_space=pltpu.VMEM)
    return pl.pallas_call(
        functools.partial(carry_kernel, n, tile),
        out_shape=jax.ShapeDtypeStruct((rows, width), jnp.float32),
        in_specs=[vmem] * 4,
        out_specs=vmem,
        scratch_shapes=[
            pltpu.VMEM((tiles, states, tile), jnp.bfloat16),
            pltpu.VMEM((tiles, states, tile), jnp.bfloat16),
            pltpu.SemaphoreType.DMA((tiles,)),
            pltpu.SemaphoreType.DMA((tiles,)),
        ],
        compiler_params=pltpu.CompilerParams(
            collective_id=0, has_side_effects=True, vmem_limit_bytes=48 * 2**20
        ),
    )(x_end, b_group.T, total, c_group)


def rotate_kernel(factor, mixed_ref, table_ref, up_ref, down_ref, out_ref):
    count = mixed_ref.shape[1] // lanes
    parts = [mixed_ref[:, i * lanes : (i + 1) * lanes] for i in range(count)]
    span = 1
    while span < count:
        for i in range(count):
            if not i & span:
                a, b = parts[i], parts[i + span]
                parts[i], parts[i + span] = a + b, a - b
        span *= 2
    table = table_ref[...]
    for i in range(count):
        at = slice(i * lanes, (i + 1) * lanes)
        upper, lower = halves(parts[i])
        rotated = (dot32(upper, table) + dot32(lower, table)) * factor
        quant = jnp.clip(rotated * up_ref[:, at], -clip_level, clip_level).astype(jnp.bfloat16)
        out_ref[:, at] = (quant.astype(jnp.float32) * down_ref[:, at]).astype(jnp.bfloat16)


def rotate(mixed, up, down):
    vmem = pl.BlockSpec(memory_space=pltpu.VMEM)
    return pl.pallas_call(
        functools.partial(rotate_kernel, 1.0 / math.sqrt(LOCAL_HEADS * P_SIZE)),
        out_shape=jax.ShapeDtypeStruct(mixed.shape, jnp.bfloat16),
        in_specs=[vmem] * 4,
        out_specs=vmem,
    )(mixed, sylvester(lanes), up[None, :], down[None, :])


def project_kernel(
    n,
    n_chan,
    n_sub,
    tile,
    scaled_ref,
    weight_hbm,
    out_ref,
    weight,
    slots,
    partial,
    slabs,
    summed,
    landed,
    local_sem,
    g_send,
    g_recv,
    s_send,
    s_recv,
    f_send,
    f_recv,
):
    me = lax.axis_index("seq")
    peers = n_chan * n_sub
    here = lax.axis_index("chan") * n_sub + lax.axis_index("sub")
    rows, feats = out_ref.shape[0], weight.shape[1]

    def slab_device(e):
        other = lax.rem(here + e, peers)
        return other, {"chan": other // n_sub, "sub": lax.rem(other, n_sub)}

    fetch = pltpu.make_async_copy(weight_hbm, weight, local_sem.at[0])
    own = pltpu.make_async_copy(scaled_ref, slots.at[me], local_sem.at[1])
    fetch.start()
    own.start()
    barrier = pltpu.get_barrier_semaphore()

    @pl.loop(1, n)
    def _(d):
        pl.semaphore_signal(
            barrier, inc=1, device_id={"seq": lax.rem(me + d, n)}, device_id_type=MESH
        )

    @pl.loop(1, peers)
    def _(e):
        pl.semaphore_signal(barrier, inc=1, device_id=slab_device(e)[1], device_id_type=MESH)

    pl.semaphore_wait(barrier, n - 1 + peers - 1)

    def block_at(s):
        return me + jnp.where(lax.rem(s, 2) == 1, -((s + 1) // 2), s // 2)

    def hop(k, way):
        return pltpu.make_async_remote_copy(
            src_ref=slots.at[k],
            dst_ref=slots.at[k],
            send_sem=g_send.at[way, k],
            recv_sem=g_recv.at[k],
            device_id={"seq": lax.rem(me + (1 if way == 1 else n - 1), n)},
            device_id_type=MESH,
        )

    def slab(k, e):
        other, device = slab_device(e)
        return pltpu.make_async_remote_copy(
            src_ref=partial.at[k, pl.ds(pl.multiple_of(other * rows, rows), rows)],
            dst_ref=slabs.at[k, e],
            send_sem=s_send.at[k, e],
            recv_sem=s_recv.at[k, e],
            device_id=device,
            device_id_type=MESH,
        )

    def finish(k, z):
        return pltpu.make_async_remote_copy(
            src_ref=summed.at[k],
            dst_ref=landed.at[me],
            send_sem=f_send.at[k],
            recv_sem=f_recv.at[z],
            device_id={"seq": k},
            device_id_type=MESH,
        )

    def when_valid(s, act):
        k = block_at(s)
        pl.when(jnp.logical_and(k >= 0, k < n))(lambda: act(k))

    own.wait()

    def pass_on(k):
        @pl.when(jnp.logical_and(k <= me, me + 1 < n))
        def _():
            hop(k, 1).start()

        @pl.when(jnp.logical_and(k >= me, me > 0))
        def _():
            hop(k, 0).start()

    pass_on(me)
    fetch.wait()

    def project_block(k):
        @pl.when(k != me)
        def _():
            hop(k, 1).wait_recv()
            pass_on(k)

        @pl.loop(0, feats // tile)
        def _(i):
            at = pl.ds(pl.multiple_of(i * tile, tile), tile)
            partial[k, :, at] = dot32(slots[k], weight[:, at]).astype(jnp.bfloat16)

        @pl.loop(1, peers)
        def _(e):
            slab(k, e).start()

    def reduce_block(k):
        @pl.loop(1, peers)
        def _(e):
            slab(k, e).wait_recv()

        mine = pl.ds(pl.multiple_of(here * rows, rows), rows)
        total = partial[k, mine, :].astype(jnp.float32)
        for e in range(1, peers):
            total = total + slabs[k, e].astype(jnp.float32)
        summed[k] = total.astype(jnp.bfloat16)

        @pl.when(k != me)
        def _():
            finish(k, me).start()

    @pl.loop(0, 2 * n - 1)
    def _(s):
        when_valid(s, project_block)

        @pl.when(s > 0)
        def _():
            when_valid(s - 1, reduce_block)

    when_valid(2 * n - 2, reduce_block)

    def columns(z):
        return pl.ds(pl.multiple_of(z * feats, feats), feats)

    out_ref[:, columns(me)] = summed[me]

    @pl.loop(1, n)
    def _(d):
        z = lax.rem(me + d, n)
        finish(z, z).wait_recv()
        out_ref[:, columns(z)] = landed[z]

    @pl.loop(1, n)
    def _(d):
        z = lax.rem(me + d, n)
        finish(z, z).wait_send()

    @pl.loop(0, n)
    def _(k):
        @pl.when(jnp.logical_and(k <= me, me + 1 < n))
        def _():
            hop(k, 1).wait_send()

        @pl.when(jnp.logical_and(k >= me, me > 0))
        def _():
            hop(k, 0).wait_send()

        @pl.loop(1, peers)
        def _(e):
            slab(k, e).wait_send()


def project(scaled, weight):
    n, n_chan, n_sub = (lax.axis_size(axis) for axis in ("seq", "chan", "sub"))
    peers = n_chan * n_sub
    rows, depth = scaled.shape
    feats = weight.shape[1]
    own_rows = rows // peers
    vmem = pl.BlockSpec(memory_space=pltpu.VMEM)
    dma = pltpu.SemaphoreType.DMA
    return pl.pallas_call(
        functools.partial(project_kernel, n, n_chan, n_sub, min(256, feats)),
        out_shape=jax.ShapeDtypeStruct((own_rows, n * feats), jnp.bfloat16),
        in_specs=[vmem, pl.BlockSpec(memory_space=pl.ANY)],
        out_specs=vmem,
        scratch_shapes=[
            pltpu.VMEM(weight.shape, jnp.bfloat16),
            pltpu.VMEM((n, rows, depth), jnp.bfloat16),
            pltpu.VMEM((n, rows, feats), jnp.bfloat16),
            pltpu.VMEM((n, peers, own_rows, feats), jnp.bfloat16),
            pltpu.VMEM((n, own_rows, feats), jnp.bfloat16),
            pltpu.VMEM((n, own_rows, feats), jnp.bfloat16),
            dma((2,)),
            dma((2, n)),
            dma((n,)),
            dma((n, peers)),
            dma((n, peers)),
            dma((n,)),
            dma((n,)),
        ],
        compiler_params=pltpu.CompilerParams(
            collective_id=1, has_side_effects=True, vmem_limit_bytes=48 * 2**20
        ),
    )(scaled, weight)


def body(
    x_in,
    b_in,
    c_in,
    step_size,
    log_decay,
    skip,
    gate_in,
    norm_gain,
    walsh_sign,
    channel_shift_power,
    out_weight,
):
    highest = lax.Precision.HIGHEST
    tok_rows, chan_width = x_in.shape
    head_local = step_size.shape[1]
    head_group = LOCAL_HEADS // G
    sub_index = lax.axis_index("sub")
    group_local = sub_index * head_local // head_group
    b_group = lax.dynamic_slice_in_dim(b_in, group_local, 1, 1)[:, 0, :]
    c_group = lax.dynamic_slice_in_dim(c_in, group_local, 1, 1)[:, 0, :]
    x_heads = x_in.astype(jnp.float32).reshape(tok_rows, head_local, P_SIZE)
    weighted = x_heads * step_size[:, :, None]
    cumul = jnp.cumsum(log_decay, axis=0)
    inner = jnp.dot(c_group, b_group.T, preferred_element_type=jnp.float32)
    differ = cumul[:, None, :] - cumul[None, :, :]
    causal = (jnp.arange(tok_rows)[:, None] >= jnp.arange(tok_rows)[None, :])[:, :, None]
    ratio = jnp.where(causal, jnp.exp(jnp.where(causal, differ, 0.0)), 0.0)
    mixing = ratio * inner[:, :, None]
    y_diag = jnp.einsum("tuh,uhp->thp", mixing, weighted, precision=highest).reshape(
        tok_rows, chan_width
    )
    to_end = jnp.exp(cumul[-1][None, :] - cumul)
    x_end = (weighted * to_end[:, :, None]).reshape(tok_rows, chan_width)
    total = jnp.repeat(cumul[-1], P_SIZE)[None, :]
    y_off = carry(x_end, b_group, total, c_group) * jnp.repeat(
        jnp.exp(cumul), P_SIZE, axis=1
    )
    y_ssm = y_diag + y_off + (x_heads * skip[None, :, None]).reshape(tok_rows, chan_width)
    gated_pre = y_ssm * jax.nn.silu(gate_in.astype(jnp.float32))
    grouped = gated_pre.reshape(tok_rows, head_local // NORM_HEADS, NORM_HEADS * P_SIZE)
    mean_sq = jnp.mean(grouped * grouped, axis=2, keepdims=True)
    gated = (
        (grouped * lax.rsqrt(mean_sq + norm_eps)).reshape(tok_rows, chan_width) * norm_gain[None, :]
    ).astype(jnp.bfloat16)
    sign_value = jnp.where(walsh_sign == 1, 1.0, -1.0).astype(jnp.bfloat16)
    signed = gated * sign_value[None, :]
    partner = partner_2(signed, "sub", 0)
    own_float = signed.astype(jnp.float32)
    partner_float = partner.astype(jnp.float32)
    mixed = jnp.where(sub_index % 2 == 1, partner_float - own_float, own_float + partner_float)
    chan_index = lax.axis_index("chan")
    for bit_index in range(lax.axis_size("chan").bit_length() - 1):
        partner = partner_2(mixed.astype(jnp.bfloat16), "chan", bit_index).astype(mixed.dtype)
        chan_bit = chan_index // 2**bit_index % 2
        mixed = jnp.where(chan_bit == 1, partner - mixed, mixed + partner)
    scaled = rotate(mixed, power_two(channel_shift_power, 1), power_two(channel_shift_power, -1))
    return project(scaled, out_weight)


def solution(mesh):
    return jax.shard_map(
        body,
        mesh=mesh,
        in_specs=(
            P(("groups", "seq"), ("chan", "sub")),
            P(("groups", "seq"), "chan", None),
            P(("groups", "seq"), "chan", None),
            P(("groups", "seq"), ("chan", "sub")),
            P(("groups", "seq"), ("chan", "sub")),
            P(("chan", "sub")),
            P(("groups", "seq"), ("chan", "sub")),
            P(("chan", "sub")),
            P(("chan", "sub")),
            P(("chan", "sub")),
            P(("chan", "sub"), "seq"),
        ),
        out_specs=P(("groups", "seq", "chan", "sub"), None),
        check_vma=False,
    )
```

```python
import functools
import math

import jax
import jax.numpy as jnp
from jax import lax
from jax.experimental import pallas as pl
from jax.experimental.pallas import tpu as pltpu
from jax.sharding import PartitionSpec as P

LOCAL_HEADS = 128
P_SIZE = 64
G = 4
NORM_HEADS = 16


norm_eps = 1e-05
clip_level = 4.0
expo_levels = (-1, 0, 1, 2, 3)
lanes = 128
MESH = pl.DeviceIdType.MESH


def partner_2(block, axis, bit):
    count = lax.axis_size(axis)
    route = []
    for low in range(count):
        high = low | 1 << bit
        if high != low and high < count:
            route += [(low, high), (high, low)]
    return lax.ppermute(block, axis, route)


def power_two(expo, sign_flip):
    result = jnp.zeros(expo.shape, jnp.float32)
    for level in expo_levels:
        result = result + jnp.where(
            expo == level, jnp.float32(2.0 ** (sign_flip * level)), jnp.float32(0.0)
        )
    return result


def sylvester(order):
    indices = jnp.arange(order, dtype=jnp.int32)
    oddness_flag = jnp.zeros((order, order), jnp.int32)
    for bit_index in range(order.bit_length() - 1):
        stride = 2**bit_index
        oddness_flag = oddness_flag + indices[:, None] // stride % 2 * (
            indices[None, :] // stride % 2
        )
    return (1 - 2 * (oddness_flag % 2)).astype(jnp.bfloat16)


def halves(value):
    upper = value.astype(jnp.bfloat16)
    return upper, (value - upper.astype(jnp.float32)).astype(jnp.bfloat16)


def dot32(left, right):
    return jnp.dot(left, right, preferred_element_type=jnp.float32)


def mixer_kernel(
    n,
    tile,
    x_ref,
    bt_ref,
    c_ref,
    cum_ref,
    step_ref,
    cumt_ref,
    stept_ref,
    skip_ref,
    y_ref,
    arrived,
    leaving,
    inner_ref,
    send,
    recv,
):
    me = lax.axis_index("seq")
    right, left = lax.rem(me + 1, n), lax.rem(me + n - 1, n)
    barrier = pltpu.get_barrier_semaphore()
    for near in (left, right):
        pl.semaphore_signal(barrier, inc=1, device_id={"seq": near}, device_id_type=MESH)

    rows, width = y_ref.shape
    tiles = width // tile
    cum = cum_ref[...]
    total = cum_ref[rows - 1 : rows, :]
    to_end = step_ref[...] * jnp.exp(total - cum)
    since = jnp.exp(cum)
    whole = jnp.exp(total)
    causal = lax.broadcasted_iota(jnp.int32, (rows, rows), 0) >= lax.broadcasted_iota(
        jnp.int32, (rows, rows), 1
    )
    inner_ref[...] = jnp.where(causal, dot32(c_ref[...], bt_ref[...]), 0.0)

    def pick(first, second):
        shape = (max(first.shape[0], second.shape[0]), lanes)
        low = lax.broadcasted_iota(jnp.int32, shape, 1) < P_SIZE
        return jnp.where(low, first, second)

    def spread(values, i):
        pairs = range(i * tile // P_SIZE, (i + 1) * tile // P_SIZE, lanes // P_SIZE)
        return jnp.concatenate(
            [pick(values[:, h : h + 1], values[:, h + 1 : h + 2]) for h in pairs], axis=1
        )

    def diagonal(h, block):
        differ = cum[:, h : h + 1] - cumt_ref[h : h + 1, :]
        mixing = jnp.exp(jnp.minimum(differ, 0.0)) * inner_ref[...] * stept_ref[h : h + 1, :]
        upper, lower = halves(mixing)
        return dot32(
            jnp.concatenate([upper, lower], axis=1), jnp.concatenate([block, block], axis=0)
        )

    def copy(i):
        return pltpu.make_async_remote_copy(
            src_ref=leaving.at[i],
            dst_ref=arrived.at[i],
            send_sem=send.at[i],
            recv_sem=recv.at[i],
            device_id={"seq": right},
            device_id_type=MESH,
        )

    pl.semaphore_wait(barrier, 2)

    for i in range(tiles):
        at = slice(i * tile, (i + 1) * tile)
        x_tile = x_ref[:, at].astype(jnp.float32)
        upper, lower = halves(x_tile * spread(to_end, i))
        own = dot32(bt_ref[...], upper) + dot32(bt_ref[...], lower)

        @pl.when(me == 0)
        def _():
            leaving[i] = own.astype(jnp.bfloat16)

        @pl.when(me > 0)
        def _():
            copy(i).wait_recv()
            leaving[i] = (arrived[i].astype(jnp.float32) * spread(whole, i) + own).astype(
                jnp.bfloat16
            )

        @pl.when(me + 1 < n)
        def _():
            copy(i).start()

        for k in range(i * tile, (i + 1) * tile, lanes):
            here = slice(k, k + lanes)
            block = x_ref[:, here]
            h = k // P_SIZE
            y_ref[:, here] = (
                pick(diagonal(h, block), diagonal(h + 1, block))
                + block.astype(jnp.float32) * skip_ref[:, here]
            )

        @pl.when(me > 0)
        def _():
            y_ref[:, at] += dot32(c_ref[...], arrived[i]) * spread(since, i)

    @pl.when(me + 1 < n)
    def _():
        for i in range(tiles):
            copy(i).wait_send()


def mixer(x_in, b_group, c_group, cumul, step_size, skip):
    n = lax.axis_size("seq")
    rows, width = x_in.shape
    tile = min(256, width)
    tiles = width // tile
    states = b_group.shape[1]
    vmem = pl.BlockSpec(memory_space=pltpu.VMEM)
    return pl.pallas_call(
        functools.partial(mixer_kernel, n, tile),
        out_shape=jax.ShapeDtypeStruct((rows, width), jnp.float32),
        in_specs=[vmem] * 8,
        out_specs=vmem,
        scratch_shapes=[
            pltpu.VMEM((tiles, states, tile), jnp.bfloat16),
            pltpu.VMEM((tiles, states, tile), jnp.bfloat16),
            pltpu.VMEM((rows, rows), jnp.float32),
            pltpu.SemaphoreType.DMA((tiles,)),
            pltpu.SemaphoreType.DMA((tiles,)),
        ],
        compiler_params=pltpu.CompilerParams(
            collective_id=0, has_side_effects=True, vmem_limit_bytes=48 * 2**20
        ),
    )(
        x_in,
        b_group.T,
        c_group,
        cumul,
        step_size,
        cumul.T,
        step_size.T,
        jnp.repeat(skip, P_SIZE)[None, :],
    )


def rotate_kernel(factor, mixed_ref, table_ref, up_ref, down_ref, out_ref):
    count = mixed_ref.shape[1] // lanes
    parts = [mixed_ref[:, i * lanes : (i + 1) * lanes] for i in range(count)]
    span = 1
    while span < count:
        for i in range(count):
            if not i & span:
                a, b = parts[i], parts[i + span]
                parts[i], parts[i + span] = a + b, a - b
        span *= 2
    table = table_ref[...]
    for i in range(count):
        at = slice(i * lanes, (i + 1) * lanes)
        upper, lower = halves(parts[i])
        rotated = (dot32(upper, table) + dot32(lower, table)) * factor
        quant = jnp.clip(rotated * up_ref[:, at], -clip_level, clip_level).astype(jnp.bfloat16)
        out_ref[:, at] = (quant.astype(jnp.float32) * down_ref[:, at]).astype(jnp.bfloat16)


def rotate(mixed, up, down):
    vmem = pl.BlockSpec(memory_space=pltpu.VMEM)
    return pl.pallas_call(
        functools.partial(rotate_kernel, 1.0 / math.sqrt(LOCAL_HEADS * P_SIZE)),
        out_shape=jax.ShapeDtypeStruct(mixed.shape, jnp.bfloat16),
        in_specs=[vmem] * 4,
        out_specs=vmem,
    )(mixed, sylvester(lanes), up[None, :], down[None, :])


def project_kernel(
    n,
    n_chan,
    n_sub,
    tile,
    scaled_ref,
    weight_hbm,
    out_ref,
    weight,
    slots,
    partial,
    slabs,
    summed,
    landed,
    local_sem,
    g_send,
    g_recv,
    s_send,
    s_recv,
    f_send,
    f_recv,
):
    me = lax.axis_index("seq")
    peers = n_chan * n_sub
    here = lax.axis_index("chan") * n_sub + lax.axis_index("sub")
    rows, feats = out_ref.shape[0], weight.shape[1]

    def slab_device(e):
        other = lax.rem(here + e, peers)
        return other, {"chan": other // n_sub, "sub": lax.rem(other, n_sub)}

    fetch = pltpu.make_async_copy(weight_hbm, weight, local_sem.at[0])
    own = pltpu.make_async_copy(scaled_ref, slots.at[me], local_sem.at[1])
    fetch.start()
    own.start()
    barrier = pltpu.get_barrier_semaphore()

    @pl.loop(1, n)
    def _(d):
        pl.semaphore_signal(
            barrier, inc=1, device_id={"seq": lax.rem(me + d, n)}, device_id_type=MESH
        )

    @pl.loop(1, peers)
    def _(e):
        pl.semaphore_signal(barrier, inc=1, device_id=slab_device(e)[1], device_id_type=MESH)

    pl.semaphore_wait(barrier, n - 1 + peers - 1)

    def block_at(s):
        return me + jnp.where(lax.rem(s, 2) == 1, -((s + 1) // 2), s // 2)

    def hop(k, way):
        return pltpu.make_async_remote_copy(
            src_ref=slots.at[k],
            dst_ref=slots.at[k],
            send_sem=g_send.at[way, k],
            recv_sem=g_recv.at[k],
            device_id={"seq": lax.rem(me + (1 if way == 1 else n - 1), n)},
            device_id_type=MESH,
        )

    def slab(k, e):
        other, device = slab_device(e)
        return pltpu.make_async_remote_copy(
            src_ref=partial.at[k, pl.ds(pl.multiple_of(other * rows, rows), rows)],
            dst_ref=slabs.at[k, e],
            send_sem=s_send.at[k, e],
            recv_sem=s_recv.at[k, e],
            device_id=device,
            device_id_type=MESH,
        )

    def finish(k, z):
        return pltpu.make_async_remote_copy(
            src_ref=summed.at[k],
            dst_ref=landed.at[me],
            send_sem=f_send.at[k],
            recv_sem=f_recv.at[z],
            device_id={"seq": k},
            device_id_type=MESH,
        )

    def when_valid(s, act):
        k = block_at(s)
        pl.when(jnp.logical_and(k >= 0, k < n))(lambda: act(k))

    own.wait()

    def pass_on(k):
        @pl.when(jnp.logical_and(k <= me, me + 1 < n))
        def _():
            hop(k, 1).start()

        @pl.when(jnp.logical_and(k >= me, me > 0))
        def _():
            hop(k, 0).start()

    pass_on(me)
    fetch.wait()

    def project_block(k):
        @pl.when(k != me)
        def _():
            hop(k, 1).wait_recv()
            pass_on(k)

        @pl.loop(0, feats // tile)
        def _(i):
            at = pl.ds(pl.multiple_of(i * tile, tile), tile)
            partial[k, :, at] = dot32(slots[k], weight[:, at]).astype(jnp.bfloat16)

        @pl.loop(1, peers)
        def _(e):
            slab(k, e).start()

    def reduce_block(k):
        @pl.loop(1, peers)
        def _(e):
            slab(k, e).wait_recv()

        mine = pl.ds(pl.multiple_of(here * rows, rows), rows)
        total = partial[k, mine, :].astype(jnp.float32)
        for e in range(1, peers):
            total = total + slabs[k, e].astype(jnp.float32)
        summed[k] = total.astype(jnp.bfloat16)

        @pl.when(k != me)
        def _():
            finish(k, me).start()

    @pl.loop(0, 2 * n - 1)
    def _(s):
        when_valid(s, project_block)

        @pl.when(s > 0)
        def _():
            when_valid(s - 1, reduce_block)

    when_valid(2 * n - 2, reduce_block)

    def columns(z):
        return pl.ds(pl.multiple_of(z * feats, feats), feats)

    out_ref[:, columns(me)] = summed[me]

    @pl.loop(1, n)
    def _(d):
        z = lax.rem(me + d, n)
        finish(z, z).wait_recv()
        out_ref[:, columns(z)] = landed[z]

    @pl.loop(1, n)
    def _(d):
        z = lax.rem(me + d, n)
        finish(z, z).wait_send()

    @pl.loop(0, n)
    def _(k):
        @pl.when(jnp.logical_and(k <= me, me + 1 < n))
        def _():
            hop(k, 1).wait_send()

        @pl.when(jnp.logical_and(k >= me, me > 0))
        def _():
            hop(k, 0).wait_send()

        @pl.loop(1, peers)
        def _(e):
            slab(k, e).wait_send()


def project(scaled, weight):
    n, n_chan, n_sub = (lax.axis_size(axis) for axis in ("seq", "chan", "sub"))
    peers = n_chan * n_sub
    rows, depth = scaled.shape
    feats = weight.shape[1]
    own_rows = rows // peers
    vmem = pl.BlockSpec(memory_space=pltpu.VMEM)
    dma = pltpu.SemaphoreType.DMA
    return pl.pallas_call(
        functools.partial(project_kernel, n, n_chan, n_sub, min(256, feats)),
        out_shape=jax.ShapeDtypeStruct((own_rows, n * feats), jnp.bfloat16),
        in_specs=[vmem, pl.BlockSpec(memory_space=pl.ANY)],
        out_specs=vmem,
        scratch_shapes=[
            pltpu.VMEM(weight.shape, jnp.bfloat16),
            pltpu.VMEM((n, rows, depth), jnp.bfloat16),
            pltpu.VMEM((n, rows, feats), jnp.bfloat16),
            pltpu.VMEM((n, peers, own_rows, feats), jnp.bfloat16),
            pltpu.VMEM((n, own_rows, feats), jnp.bfloat16),
            pltpu.VMEM((n, own_rows, feats), jnp.bfloat16),
            dma((2,)),
            dma((2, n)),
            dma((n,)),
            dma((n, peers)),
            dma((n, peers)),
            dma((n,)),
            dma((n,)),
        ],
        compiler_params=pltpu.CompilerParams(
            collective_id=1, has_side_effects=True, vmem_limit_bytes=60 * 2**20
        ),
    )(scaled, weight)


def body(
    x_in,
    b_in,
    c_in,
    step_size,
    log_decay,
    skip,
    gate_in,
    norm_gain,
    walsh_sign,
    channel_shift_power,
    out_weight,
):
    tok_rows, chan_width = x_in.shape
    head_local = step_size.shape[1]
    head_group = LOCAL_HEADS // G
    sub_index = lax.axis_index("sub")
    group_local = sub_index * head_local // head_group
    b_group = lax.dynamic_slice_in_dim(b_in, group_local, 1, 1)[:, 0, :]
    c_group = lax.dynamic_slice_in_dim(c_in, group_local, 1, 1)[:, 0, :]
    y_ssm = mixer(x_in, b_group, c_group, jnp.cumsum(log_decay, axis=0), step_size, skip)
    gated_pre = y_ssm * jax.nn.silu(gate_in.astype(jnp.float32))
    grouped = gated_pre.reshape(tok_rows, head_local // NORM_HEADS, NORM_HEADS * P_SIZE)
    mean_sq = jnp.mean(grouped * grouped, axis=2, keepdims=True)
    gated = (
        (grouped * lax.rsqrt(mean_sq + norm_eps)).reshape(tok_rows, chan_width) * norm_gain[None, :]
    ).astype(jnp.bfloat16)
    sign_value = jnp.where(walsh_sign == 1, 1.0, -1.0).astype(jnp.bfloat16)
    signed = gated * sign_value[None, :]
    partner = partner_2(signed, "sub", 0)
    own_float = signed.astype(jnp.float32)
    partner_float = partner.astype(jnp.float32)
    mixed = jnp.where(sub_index % 2 == 1, partner_float - own_float, own_float + partner_float)
    chan_index = lax.axis_index("chan")
    for bit_index in range(lax.axis_size("chan").bit_length() - 1):
        partner = partner_2(mixed.astype(jnp.bfloat16), "chan", bit_index).astype(mixed.dtype)
        chan_bit = chan_index // 2**bit_index % 2
        mixed = jnp.where(chan_bit == 1, partner - mixed, mixed + partner)
    scaled = rotate(mixed, power_two(channel_shift_power, 1), power_two(channel_shift_power, -1))
    return project(scaled, out_weight)


def solution(mesh):
    return jax.shard_map(
        body,
        mesh=mesh,
        in_specs=(
            P(("groups", "seq"), ("chan", "sub")),
            P(("groups", "seq"), "chan", None),
            P(("groups", "seq"), "chan", None),
            P(("groups", "seq"), ("chan", "sub")),
            P(("groups", "seq"), ("chan", "sub")),
            P(("chan", "sub")),
            P(("groups", "seq"), ("chan", "sub")),
            P(("chan", "sub")),
            P(("chan", "sub")),
            P(("chan", "sub")),
            P(("chan", "sub"), "seq"),
        ),
        out_specs=P(("groups", "seq", "chan", "sub"), None),
        check_vma=False,
    )
```

```python
import functools
import math

import jax
import jax.numpy as jnp
from jax import lax
from jax.experimental import pallas as pl
from jax.experimental.pallas import tpu as pltpu
from jax.sharding import PartitionSpec as P

LOCAL_HEADS = 128
P_SIZE = 64
G = 4
NORM_HEADS = 16


norm_eps = 1e-05
clip_level = 4.0
expo_levels = (-1, 0, 1, 2, 3)
lanes = 128
pieces = 2
MESH = pl.DeviceIdType.MESH


def partner_2(block, axis, bit):
    count = lax.axis_size(axis)
    route = []
    for low in range(count):
        high = low | 1 << bit
        if high != low and high < count:
            route += [(low, high), (high, low)]
    return lax.ppermute(block, axis, route)


def power_two(expo, sign_flip):
    result = jnp.zeros(expo.shape, jnp.float32)
    for level in expo_levels:
        result = result + jnp.where(
            expo == level, jnp.float32(2.0 ** (sign_flip * level)), jnp.float32(0.0)
        )
    return result


def sylvester(order):
    indices = jnp.arange(order, dtype=jnp.int32)
    oddness_flag = jnp.zeros((order, order), jnp.int32)
    for bit_index in range(order.bit_length() - 1):
        stride = 2**bit_index
        oddness_flag = oddness_flag + indices[:, None] // stride % 2 * (
            indices[None, :] // stride % 2
        )
    return (1 - 2 * (oddness_flag % 2)).astype(jnp.bfloat16)


def halves(value):
    upper = value.astype(jnp.bfloat16)
    return upper, (value - upper.astype(jnp.float32)).astype(jnp.bfloat16)


def dot32(left, right):
    return jnp.dot(left, right, preferred_element_type=jnp.float32)


def mixer_kernel(
    n,
    tile,
    x_ref,
    bt_ref,
    c_ref,
    cum_ref,
    step_ref,
    cumt_ref,
    stept_ref,
    skip_ref,
    y_ref,
    arrived,
    leaving,
    inner_ref,
    send,
    recv,
):
    me = lax.axis_index("seq")
    right, left = lax.rem(me + 1, n), lax.rem(me + n - 1, n)
    barrier = pltpu.get_barrier_semaphore()
    for near in (left, right):
        pl.semaphore_signal(barrier, inc=1, device_id={"seq": near}, device_id_type=MESH)

    rows, width = y_ref.shape
    tiles = width // tile
    cum = cum_ref[...]
    total = cum_ref[rows - 1 : rows, :]
    to_end = step_ref[...] * jnp.exp(total - cum)
    since = jnp.exp(cum)
    whole = jnp.exp(total)
    causal = lax.broadcasted_iota(jnp.int32, (rows, rows), 0) >= lax.broadcasted_iota(
        jnp.int32, (rows, rows), 1
    )
    inner_ref[...] = jnp.where(causal, dot32(c_ref[...], bt_ref[...]), 0.0)

    def pick(first, second):
        shape = (max(first.shape[0], second.shape[0]), lanes)
        low = lax.broadcasted_iota(jnp.int32, shape, 1) < P_SIZE
        return jnp.where(low, first, second)

    def spread(values, i):
        pairs = range(i * tile // P_SIZE, (i + 1) * tile // P_SIZE, lanes // P_SIZE)
        return jnp.concatenate(
            [pick(values[:, h : h + 1], values[:, h + 1 : h + 2]) for h in pairs], axis=1
        )

    def diagonal(h, block):
        differ = cum[:, h : h + 1] - cumt_ref[h : h + 1, :]
        mixing = jnp.exp(jnp.minimum(differ, 0.0)) * inner_ref[...] * stept_ref[h : h + 1, :]
        upper, lower = halves(mixing)
        return dot32(
            jnp.concatenate([upper, lower], axis=1), jnp.concatenate([block, block], axis=0)
        )

    def copy(i):
        return pltpu.make_async_remote_copy(
            src_ref=leaving.at[i],
            dst_ref=arrived.at[i],
            send_sem=send.at[i],
            recv_sem=recv.at[i],
            device_id={"seq": right},
            device_id_type=MESH,
        )

    pl.semaphore_wait(barrier, 2)

    for i in range(tiles):
        at = slice(i * tile, (i + 1) * tile)
        x_tile = x_ref[:, at].astype(jnp.float32)
        upper, lower = halves(x_tile * spread(to_end, i))
        own = dot32(bt_ref[...], upper) + dot32(bt_ref[...], lower)

        @pl.when(me == 0)
        def _():
            leaving[i] = own.astype(jnp.bfloat16)

        @pl.when(me > 0)
        def _():
            copy(i).wait_recv()
            leaving[i] = (arrived[i].astype(jnp.float32) * spread(whole, i) + own).astype(
                jnp.bfloat16
            )

        @pl.when(me + 1 < n)
        def _():
            copy(i).start()

        for k in range(i * tile, (i + 1) * tile, lanes):
            here = slice(k, k + lanes)
            block = x_ref[:, here]
            h = k // P_SIZE
            y_ref[:, here] = (
                pick(diagonal(h, block), diagonal(h + 1, block))
                + block.astype(jnp.float32) * skip_ref[:, here]
            )

        @pl.when(me > 0)
        def _():
            y_ref[:, at] += dot32(c_ref[...], arrived[i]) * spread(since, i)

    @pl.when(me + 1 < n)
    def _():
        for i in range(tiles):
            copy(i).wait_send()


def mixer(x_in, b_group, c_group, cumul, step_size, skip):
    n = lax.axis_size("seq")
    rows, width = x_in.shape
    tile = min(256, width)
    tiles = width // tile
    states = b_group.shape[1]
    vmem = pl.BlockSpec(memory_space=pltpu.VMEM)
    return pl.pallas_call(
        functools.partial(mixer_kernel, n, tile),
        out_shape=jax.ShapeDtypeStruct((rows, width), jnp.float32),
        in_specs=[vmem] * 8,
        out_specs=vmem,
        scratch_shapes=[
            pltpu.VMEM((tiles, states, tile), jnp.bfloat16),
            pltpu.VMEM((tiles, states, tile), jnp.bfloat16),
            pltpu.VMEM((rows, rows), jnp.float32),
            pltpu.SemaphoreType.DMA((tiles,)),
            pltpu.SemaphoreType.DMA((tiles,)),
        ],
        compiler_params=pltpu.CompilerParams(
            collective_id=0, has_side_effects=True, vmem_limit_bytes=48 * 2**20
        ),
    )(
        x_in,
        b_group.T,
        c_group,
        cumul,
        step_size,
        cumul.T,
        step_size.T,
        jnp.repeat(skip, P_SIZE)[None, :],
    )


def rotate_kernel(factor, mixed_ref, table_ref, up_ref, down_ref, out_ref):
    count = mixed_ref.shape[1] // lanes
    parts = [mixed_ref[:, i * lanes : (i + 1) * lanes] for i in range(count)]
    span = 1
    while span < count:
        for i in range(count):
            if not i & span:
                a, b = parts[i], parts[i + span]
                parts[i], parts[i + span] = a + b, a - b
        span *= 2
    table = table_ref[...]
    for i in range(count):
        at = slice(i * lanes, (i + 1) * lanes)
        upper, lower = halves(parts[i])
        rotated = (dot32(upper, table) + dot32(lower, table)) * factor
        quant = jnp.clip(rotated * up_ref[:, at], -clip_level, clip_level).astype(jnp.bfloat16)
        out_ref[:, at] = (quant.astype(jnp.float32) * down_ref[:, at]).astype(jnp.bfloat16)


def rotate(mixed, up, down):
    vmem = pl.BlockSpec(memory_space=pltpu.VMEM)
    return pl.pallas_call(
        functools.partial(rotate_kernel, 1.0 / math.sqrt(LOCAL_HEADS * P_SIZE)),
        out_shape=jax.ShapeDtypeStruct(mixed.shape, jnp.bfloat16),
        in_specs=[vmem] * 4,
        out_specs=vmem,
    )(mixed, sylvester(lanes), up[None, :], down[None, :])


def project_kernel(
    n,
    n_chan,
    n_sub,
    tile,
    scaled_ref,
    weight_hbm,
    out_ref,
    weight,
    slots,
    partial,
    slabs,
    summed,
    landed,
    local_sem,
    g_send,
    g_recv,
    s_send,
    s_recv,
    f_send,
    f_recv,
):
    me = lax.axis_index("seq")
    peers = n_chan * n_sub
    here = lax.axis_index("chan") * n_sub + lax.axis_index("sub")
    rows, feats = out_ref.shape[0], weight.shape[1]

    def slab_device(e):
        other = lax.rem(here + e, peers)
        return other, {"chan": other // n_sub, "sub": lax.rem(other, n_sub)}

    fetch = pltpu.make_async_copy(weight_hbm, weight, local_sem.at[0])
    own = pltpu.make_async_copy(scaled_ref, slots.at[me], local_sem.at[1])
    fetch.start()
    own.start()
    barrier = pltpu.get_barrier_semaphore()

    @pl.loop(1, n)
    def _(d):
        pl.semaphore_signal(
            barrier, inc=1, device_id={"seq": lax.rem(me + d, n)}, device_id_type=MESH
        )

    @pl.loop(1, peers)
    def _(e):
        pl.semaphore_signal(barrier, inc=1, device_id=slab_device(e)[1], device_id_type=MESH)

    pl.semaphore_wait(barrier, n - 1 + peers - 1)

    piece = slots.shape[1] // pieces

    def hop(k, q, way):
        return pltpu.make_async_remote_copy(
            src_ref=slots.at[k, pl.ds(q * piece, piece)],
            dst_ref=slots.at[k, pl.ds(q * piece, piece)],
            send_sem=g_send.at[way, k, q],
            recv_sem=g_recv.at[k, q],
            device_id={"seq": lax.rem(me + (1 if way == 1 else n - 1), n)},
            device_id_type=MESH,
        )

    def slab(k, e):
        other, device = slab_device(e)
        return pltpu.make_async_remote_copy(
            src_ref=partial.at[k, pl.ds(pl.multiple_of(other * rows, rows), rows)],
            dst_ref=slabs.at[k, e],
            send_sem=s_send.at[k, e],
            recv_sem=s_recv.at[k, e],
            device_id=device,
            device_id_type=MESH,
        )

    def finish(k, z):
        return pltpu.make_async_remote_copy(
            src_ref=summed.at[k],
            dst_ref=landed.at[me],
            send_sem=f_send.at[k],
            recv_sem=f_recv.at[z],
            device_id={"seq": k},
            device_id_type=MESH,
        )

    def when_valid(k, act):
        pl.when(jnp.logical_and(k >= 0, k < n))(lambda: act(k))

    def to_right(k, q):
        @pl.when(me + 1 < n)
        def _():
            hop(k, q, 1).start()

    def to_left(k, q):
        @pl.when(me > 0)
        def _():
            hop(k, q, 0).start()

    own.wait()
    for q in range(pieces):
        to_right(me, q)
        to_left(me, q)
    fetch.wait()

    def project_block(k):
        @pl.loop(0, feats // tile)
        def _(i):
            at = pl.ds(pl.multiple_of(i * tile, tile), tile)
            partial[k, :, at] = dot32(slots[k], weight[:, at]).astype(jnp.bfloat16)

        @pl.loop(1, peers)
        def _(e):
            slab(k, e).start()

    def reduce_block(k):
        @pl.loop(1, peers)
        def _(e):
            slab(k, e).wait_recv()

        mine = pl.ds(pl.multiple_of(here * rows, rows), rows)
        total = partial[k, mine, :].astype(jnp.float32)
        for e in range(1, peers):
            total = total + slabs[k, e].astype(jnp.float32)
        summed[k] = total.astype(jnp.bfloat16)

        @pl.when(k != me)
        def _():
            finish(k, me).start()

    project_block(me)

    @pl.loop(1, n)
    def _(j):
        for q in range(pieces):

            def from_left(k, q=q):
                hop(k, q, 1).wait_recv()
                to_right(k, q)

            def from_right(k, q=q):
                hop(k, q, 0).wait_recv()
                to_left(k, q)

            when_valid(me - j, from_left)
            when_valid(me + j, from_right)

        when_valid(me - j, project_block)
        when_valid(me + j, project_block)

        @pl.when(j == 1)
        def _():
            reduce_block(me)

        @pl.when(j > 1)
        def _():
            when_valid(me - j + 1, reduce_block)
            when_valid(me + j - 1, reduce_block)

    when_valid(me - n + 1, reduce_block)
    when_valid(me + n - 1, reduce_block)

    def columns(z):
        return pl.ds(pl.multiple_of(z * feats, feats), feats)

    out_ref[:, columns(me)] = summed[me]

    @pl.loop(1, n)
    def _(d):
        z = lax.rem(me + d, n)
        finish(z, z).wait_recv()
        out_ref[:, columns(z)] = landed[z]

    @pl.loop(1, n)
    def _(d):
        z = lax.rem(me + d, n)
        finish(z, z).wait_send()

    @pl.loop(0, n)
    def _(k):
        @pl.when(jnp.logical_and(k <= me, me + 1 < n))
        def _():
            for q in range(pieces):
                hop(k, q, 1).wait_send()

        @pl.when(jnp.logical_and(k >= me, me > 0))
        def _():
            for q in range(pieces):
                hop(k, q, 0).wait_send()

        @pl.loop(1, peers)
        def _(e):
            slab(k, e).wait_send()


def project(scaled, weight):
    n, n_chan, n_sub = (lax.axis_size(axis) for axis in ("seq", "chan", "sub"))
    peers = n_chan * n_sub
    rows, depth = scaled.shape
    feats = weight.shape[1]
    own_rows = rows // peers
    vmem = pl.BlockSpec(memory_space=pltpu.VMEM)
    dma = pltpu.SemaphoreType.DMA
    return pl.pallas_call(
        functools.partial(project_kernel, n, n_chan, n_sub, min(256, feats)),
        out_shape=jax.ShapeDtypeStruct((own_rows, n * feats), jnp.bfloat16),
        in_specs=[vmem, pl.BlockSpec(memory_space=pl.ANY)],
        out_specs=vmem,
        scratch_shapes=[
            pltpu.VMEM(weight.shape, jnp.bfloat16),
            pltpu.VMEM((n, rows, depth), jnp.bfloat16),
            pltpu.VMEM((n, rows, feats), jnp.bfloat16),
            pltpu.VMEM((n, peers, own_rows, feats), jnp.bfloat16),
            pltpu.VMEM((n, own_rows, feats), jnp.bfloat16),
            pltpu.VMEM((n, own_rows, feats), jnp.bfloat16),
            dma((2,)),
            dma((2, n, pieces)),
            dma((n, pieces)),
            dma((n, peers)),
            dma((n, peers)),
            dma((n,)),
            dma((n,)),
        ],
        compiler_params=pltpu.CompilerParams(
            collective_id=1, has_side_effects=True, vmem_limit_bytes=60 * 2**20
        ),
    )(scaled, weight)


def body(
    x_in,
    b_in,
    c_in,
    step_size,
    log_decay,
    skip,
    gate_in,
    norm_gain,
    walsh_sign,
    channel_shift_power,
    out_weight,
):
    tok_rows, chan_width = x_in.shape
    head_local = step_size.shape[1]
    head_group = LOCAL_HEADS // G
    sub_index = lax.axis_index("sub")
    group_local = sub_index * head_local // head_group
    b_group = lax.dynamic_slice_in_dim(b_in, group_local, 1, 1)[:, 0, :]
    c_group = lax.dynamic_slice_in_dim(c_in, group_local, 1, 1)[:, 0, :]
    y_ssm = mixer(x_in, b_group, c_group, jnp.cumsum(log_decay, axis=0), step_size, skip)
    gated_pre = y_ssm * jax.nn.silu(gate_in.astype(jnp.float32))
    grouped = gated_pre.reshape(tok_rows, head_local // NORM_HEADS, NORM_HEADS * P_SIZE)
    mean_sq = jnp.mean(grouped * grouped, axis=2, keepdims=True)
    gated = (
        (grouped * lax.rsqrt(mean_sq + norm_eps)).reshape(tok_rows, chan_width) * norm_gain[None, :]
    ).astype(jnp.bfloat16)
    sign_value = jnp.where(walsh_sign == 1, 1.0, -1.0).astype(jnp.bfloat16)
    signed = gated * sign_value[None, :]
    partner = partner_2(signed, "sub", 0)
    own_float = signed.astype(jnp.float32)
    partner_float = partner.astype(jnp.float32)
    mixed = jnp.where(sub_index % 2 == 1, partner_float - own_float, own_float + partner_float)
    chan_index = lax.axis_index("chan")
    for bit_index in range(lax.axis_size("chan").bit_length() - 1):
        partner = partner_2(mixed.astype(jnp.bfloat16), "chan", bit_index).astype(mixed.dtype)
        chan_bit = chan_index // 2**bit_index % 2
        mixed = jnp.where(chan_bit == 1, partner - mixed, mixed + partner)
    scaled = rotate(mixed, power_two(channel_shift_power, 1), power_two(channel_shift_power, -1))
    return project(scaled, out_weight)


def solution(mesh):
    return jax.shard_map(
        body,
        mesh=mesh,
        in_specs=(
            P(("groups", "seq"), ("chan", "sub")),
            P(("groups", "seq"), "chan", None),
            P(("groups", "seq"), "chan", None),
            P(("groups", "seq"), ("chan", "sub")),
            P(("groups", "seq"), ("chan", "sub")),
            P(("chan", "sub")),
            P(("groups", "seq"), ("chan", "sub")),
            P(("chan", "sub")),
            P(("chan", "sub")),
            P(("chan", "sub")),
            P(("chan", "sub"), "seq"),
        ),
        out_specs=P(("groups", "seq", "chan", "sub"), None),
        check_vma=False,
    )
```

```python
import functools
import math

import jax
import jax.numpy as jnp
from jax import lax
from jax.experimental import pallas as pl
from jax.experimental.pallas import tpu as pltpu
from jax.sharding import PartitionSpec as P

LOCAL_HEADS = 128
P_SIZE = 64
G = 4
NORM_HEADS = 16


norm_eps = 1e-05
clip_level = 4.0
expo_levels = (-1, 0, 1, 2, 3)
lanes = 128
pieces = 4
MESH = pl.DeviceIdType.MESH


def partner_2(block, axis, bit):
    count = lax.axis_size(axis)
    route = []
    for low in range(count):
        high = low | 1 << bit
        if high != low and high < count:
            route += [(low, high), (high, low)]
    return lax.ppermute(block, axis, route)


def power_two(expo, sign_flip):
    result = jnp.zeros(expo.shape, jnp.float32)
    for level in expo_levels:
        result = result + jnp.where(
            expo == level, jnp.float32(2.0 ** (sign_flip * level)), jnp.float32(0.0)
        )
    return result


def sylvester(order):
    indices = jnp.arange(order, dtype=jnp.int32)
    oddness_flag = jnp.zeros((order, order), jnp.int32)
    for bit_index in range(order.bit_length() - 1):
        stride = 2**bit_index
        oddness_flag = oddness_flag + indices[:, None] // stride % 2 * (
            indices[None, :] // stride % 2
        )
    return (1 - 2 * (oddness_flag % 2)).astype(jnp.bfloat16)


def halves(value):
    upper = value.astype(jnp.bfloat16)
    return upper, (value - upper.astype(jnp.float32)).astype(jnp.bfloat16)


def dot32(left, right):
    return jnp.dot(left, right, preferred_element_type=jnp.float32)


def mixer_kernel(
    n,
    tile,
    x_ref,
    bt_ref,
    c_ref,
    cum_ref,
    step_ref,
    cumt_ref,
    stept_ref,
    skip_ref,
    y_ref,
    arrived,
    leaving,
    inner_ref,
    send,
    recv,
):
    me = lax.axis_index("seq")
    right, left = lax.rem(me + 1, n), lax.rem(me + n - 1, n)
    barrier = pltpu.get_barrier_semaphore()
    for near in (left, right):
        pl.semaphore_signal(barrier, inc=1, device_id={"seq": near}, device_id_type=MESH)

    rows, width = y_ref.shape
    tiles = width // tile
    cum = cum_ref[...]
    total = cum_ref[rows - 1 : rows, :]
    to_end = step_ref[...] * jnp.exp(total - cum)
    since = jnp.exp(cum)
    whole = jnp.exp(total)
    causal = lax.broadcasted_iota(jnp.int32, (rows, rows), 0) >= lax.broadcasted_iota(
        jnp.int32, (rows, rows), 1
    )
    inner_ref[...] = jnp.where(causal, dot32(c_ref[...], bt_ref[...]), 0.0)

    def pick(first, second):
        shape = (max(first.shape[0], second.shape[0]), lanes)
        low = lax.broadcasted_iota(jnp.int32, shape, 1) < P_SIZE
        return jnp.where(low, first, second)

    def spread(values, i):
        pairs = range(i * tile // P_SIZE, (i + 1) * tile // P_SIZE, lanes // P_SIZE)
        return jnp.concatenate(
            [pick(values[:, h : h + 1], values[:, h + 1 : h + 2]) for h in pairs], axis=1
        )

    def diagonal(h, block):
        differ = cum[:, h : h + 1] - cumt_ref[h : h + 1, :]
        mixing = jnp.exp(jnp.minimum(differ, 0.0)) * inner_ref[...] * stept_ref[h : h + 1, :]
        upper, lower = halves(mixing)
        return dot32(
            jnp.concatenate([upper, lower], axis=1), jnp.concatenate([block, block], axis=0)
        )

    def copy(i):
        return pltpu.make_async_remote_copy(
            src_ref=leaving.at[i],
            dst_ref=arrived.at[i],
            send_sem=send.at[i],
            recv_sem=recv.at[i],
            device_id={"seq": right},
            device_id_type=MESH,
        )

    pl.semaphore_wait(barrier, 2)

    for i in range(tiles):
        at = slice(i * tile, (i + 1) * tile)
        x_tile = x_ref[:, at].astype(jnp.float32)
        upper, lower = halves(x_tile * spread(to_end, i))
        own = dot32(bt_ref[...], upper) + dot32(bt_ref[...], lower)

        @pl.when(me == 0)
        def _():
            leaving[i] = own.astype(jnp.bfloat16)

        @pl.when(me > 0)
        def _():
            copy(i).wait_recv()
            leaving[i] = (arrived[i].astype(jnp.float32) * spread(whole, i) + own).astype(
                jnp.bfloat16
            )

        @pl.when(me + 1 < n)
        def _():
            copy(i).start()

        for k in range(i * tile, (i + 1) * tile, lanes):
            here = slice(k, k + lanes)
            block = x_ref[:, here]
            h = k // P_SIZE
            y_ref[:, here] = (
                pick(diagonal(h, block), diagonal(h + 1, block))
                + block.astype(jnp.float32) * skip_ref[:, here]
            )

        @pl.when(me > 0)
        def _():
            y_ref[:, at] += dot32(c_ref[...], arrived[i]) * spread(since, i)

    @pl.when(me + 1 < n)
    def _():
        for i in range(tiles):
            copy(i).wait_send()


def mixer(x_in, b_group, c_group, cumul, step_size, skip):
    n = lax.axis_size("seq")
    rows, width = x_in.shape
    tile = min(128, width)
    tiles = width // tile
    states = b_group.shape[1]
    vmem = pl.BlockSpec(memory_space=pltpu.VMEM)
    return pl.pallas_call(
        functools.partial(mixer_kernel, n, tile),
        out_shape=jax.ShapeDtypeStruct((rows, width), jnp.float32),
        in_specs=[vmem] * 8,
        out_specs=vmem,
        scratch_shapes=[
            pltpu.VMEM((tiles, states, tile), jnp.bfloat16),
            pltpu.VMEM((tiles, states, tile), jnp.bfloat16),
            pltpu.VMEM((rows, rows), jnp.float32),
            pltpu.SemaphoreType.DMA((tiles,)),
            pltpu.SemaphoreType.DMA((tiles,)),
        ],
        compiler_params=pltpu.CompilerParams(
            collective_id=0, has_side_effects=True, vmem_limit_bytes=48 * 2**20
        ),
    )(
        x_in,
        b_group.T,
        c_group,
        cumul,
        step_size,
        cumul.T,
        step_size.T,
        jnp.repeat(skip, P_SIZE)[None, :],
    )


def rotate_kernel(factor, mixed_ref, table_ref, up_ref, down_ref, out_ref):
    count = mixed_ref.shape[1] // lanes
    parts = [mixed_ref[:, i * lanes : (i + 1) * lanes] for i in range(count)]
    span = 1
    while span < count:
        for i in range(count):
            if not i & span:
                a, b = parts[i], parts[i + span]
                parts[i], parts[i + span] = a + b, a - b
        span *= 2
    table = table_ref[...]
    for i in range(count):
        at = slice(i * lanes, (i + 1) * lanes)
        upper, lower = halves(parts[i])
        rotated = (dot32(upper, table) + dot32(lower, table)) * factor
        quant = jnp.clip(rotated * up_ref[:, at], -clip_level, clip_level).astype(jnp.bfloat16)
        out_ref[:, at] = (quant.astype(jnp.float32) * down_ref[:, at]).astype(jnp.bfloat16)


def rotate(mixed, up, down):
    vmem = pl.BlockSpec(memory_space=pltpu.VMEM)
    return pl.pallas_call(
        functools.partial(rotate_kernel, 1.0 / math.sqrt(LOCAL_HEADS * P_SIZE)),
        out_shape=jax.ShapeDtypeStruct(mixed.shape, jnp.bfloat16),
        in_specs=[vmem] * 4,
        out_specs=vmem,
    )(mixed, sylvester(lanes), up[None, :], down[None, :])


def project_kernel(
    n,
    n_chan,
    n_sub,
    tile,
    scaled_ref,
    weight_hbm,
    out_ref,
    weight,
    slots,
    partial,
    slabs,
    summed,
    landed,
    local_sem,
    g_send,
    g_recv,
    s_send,
    s_recv,
    f_send,
    f_recv,
):
    me = lax.axis_index("seq")
    peers = n_chan * n_sub
    here = lax.axis_index("chan") * n_sub + lax.axis_index("sub")
    rows, feats = out_ref.shape[0], weight.shape[1]

    def slab_device(e):
        other = lax.rem(here + e, peers)
        return other, {"chan": other // n_sub, "sub": lax.rem(other, n_sub)}

    fetch = pltpu.make_async_copy(weight_hbm, weight, local_sem.at[0])
    own = pltpu.make_async_copy(scaled_ref, slots.at[me], local_sem.at[1])
    fetch.start()
    own.start()
    barrier = pltpu.get_barrier_semaphore()

    @pl.loop(1, n)
    def _(d):
        pl.semaphore_signal(
            barrier, inc=1, device_id={"seq": lax.rem(me + d, n)}, device_id_type=MESH
        )

    @pl.loop(1, peers)
    def _(e):
        pl.semaphore_signal(barrier, inc=1, device_id=slab_device(e)[1], device_id_type=MESH)

    pl.semaphore_wait(barrier, n - 1 + peers - 1)

    piece = slots.shape[1] // pieces

    def hop(k, q, way):
        return pltpu.make_async_remote_copy(
            src_ref=slots.at[k, pl.ds(q * piece, piece)],
            dst_ref=slots.at[k, pl.ds(q * piece, piece)],
            send_sem=g_send.at[way, k, q],
            recv_sem=g_recv.at[k, q],
            device_id={"seq": lax.rem(me + (1 if way == 1 else n - 1), n)},
            device_id_type=MESH,
        )

    def slab(k, e):
        other, device = slab_device(e)
        return pltpu.make_async_remote_copy(
            src_ref=partial.at[k, pl.ds(pl.multiple_of(other * rows, rows), rows)],
            dst_ref=slabs.at[k, e],
            send_sem=s_send.at[k, e],
            recv_sem=s_recv.at[k, e],
            device_id=device,
            device_id_type=MESH,
        )

    def finish(k, z):
        return pltpu.make_async_remote_copy(
            src_ref=summed.at[k],
            dst_ref=landed.at[me],
            send_sem=f_send.at[k],
            recv_sem=f_recv.at[z],
            device_id={"seq": k},
            device_id_type=MESH,
        )

    def when_valid(k, act):
        pl.when(jnp.logical_and(k >= 0, k < n))(lambda: act(k))

    def to_right(k, q):
        @pl.when(me + 1 < n)
        def _():
            hop(k, q, 1).start()

    def to_left(k, q):
        @pl.when(me > 0)
        def _():
            hop(k, q, 0).start()

    own.wait()
    for q in range(pieces):
        to_right(me, q)
        to_left(me, q)
    fetch.wait()

    def project_block(k):
        @pl.loop(0, feats // tile)
        def _(i):
            at = pl.ds(pl.multiple_of(i * tile, tile), tile)
            partial[k, :, at] = dot32(slots[k], weight[:, at]).astype(jnp.bfloat16)

        @pl.loop(1, peers)
        def _(e):
            slab(k, e).start()

    def reduce_block(k):
        @pl.loop(1, peers)
        def _(e):
            slab(k, e).wait_recv()

        mine = pl.ds(pl.multiple_of(here * rows, rows), rows)
        total = partial[k, mine, :].astype(jnp.float32)
        for e in range(1, peers):
            total = total + slabs[k, e].astype(jnp.float32)
        summed[k] = total.astype(jnp.bfloat16)

        @pl.when(k != me)
        def _():
            finish(k, me).start()

    project_block(me)

    @pl.loop(1, n)
    def _(j):
        for q in range(pieces):

            def from_left(k, q=q):
                hop(k, q, 1).wait_recv()
                to_right(k, q)

            def from_right(k, q=q):
                hop(k, q, 0).wait_recv()
                to_left(k, q)

            when_valid(me - j, from_left)
            when_valid(me + j, from_right)

        when_valid(me - j, project_block)
        when_valid(me + j, project_block)

        @pl.when(j == 1)
        def _():
            reduce_block(me)

        @pl.when(j > 1)
        def _():
            when_valid(me - j + 1, reduce_block)
            when_valid(me + j - 1, reduce_block)

    when_valid(me - n + 1, reduce_block)
    when_valid(me + n - 1, reduce_block)

    def columns(z):
        return pl.ds(pl.multiple_of(z * feats, feats), feats)

    out_ref[:, columns(me)] = summed[me]

    @pl.loop(1, n)
    def _(d):
        z = lax.rem(me + d, n)
        finish(z, z).wait_recv()
        out_ref[:, columns(z)] = landed[z]

    @pl.loop(1, n)
    def _(d):
        z = lax.rem(me + d, n)
        finish(z, z).wait_send()

    @pl.loop(0, n)
    def _(k):
        @pl.when(jnp.logical_and(k <= me, me + 1 < n))
        def _():
            for q in range(pieces):
                hop(k, q, 1).wait_send()

        @pl.when(jnp.logical_and(k >= me, me > 0))
        def _():
            for q in range(pieces):
                hop(k, q, 0).wait_send()

        @pl.loop(1, peers)
        def _(e):
            slab(k, e).wait_send()


def project(scaled, weight):
    n, n_chan, n_sub = (lax.axis_size(axis) for axis in ("seq", "chan", "sub"))
    peers = n_chan * n_sub
    rows, depth = scaled.shape
    feats = weight.shape[1]
    own_rows = rows // peers
    vmem = pl.BlockSpec(memory_space=pltpu.VMEM)
    dma = pltpu.SemaphoreType.DMA
    return pl.pallas_call(
        functools.partial(project_kernel, n, n_chan, n_sub, min(256, feats)),
        out_shape=jax.ShapeDtypeStruct((own_rows, n * feats), jnp.bfloat16),
        in_specs=[vmem, pl.BlockSpec(memory_space=pl.ANY)],
        out_specs=vmem,
        scratch_shapes=[
            pltpu.VMEM(weight.shape, jnp.bfloat16),
            pltpu.VMEM((n, rows, depth), jnp.bfloat16),
            pltpu.VMEM((n, rows, feats), jnp.bfloat16),
            pltpu.VMEM((n, peers, own_rows, feats), jnp.bfloat16),
            pltpu.VMEM((n, own_rows, feats), jnp.bfloat16),
            pltpu.VMEM((n, own_rows, feats), jnp.bfloat16),
            dma((2,)),
            dma((2, n, pieces)),
            dma((n, pieces)),
            dma((n, peers)),
            dma((n, peers)),
            dma((n,)),
            dma((n,)),
        ],
        compiler_params=pltpu.CompilerParams(
            collective_id=1, has_side_effects=True, vmem_limit_bytes=60 * 2**20
        ),
    )(scaled, weight)


def body(
    x_in,
    b_in,
    c_in,
    step_size,
    log_decay,
    skip,
    gate_in,
    norm_gain,
    walsh_sign,
    channel_shift_power,
    out_weight,
):
    tok_rows, chan_width = x_in.shape
    head_local = step_size.shape[1]
    head_group = LOCAL_HEADS // G
    sub_index = lax.axis_index("sub")
    group_local = sub_index * head_local // head_group
    b_group = lax.dynamic_slice_in_dim(b_in, group_local, 1, 1)[:, 0, :]
    c_group = lax.dynamic_slice_in_dim(c_in, group_local, 1, 1)[:, 0, :]
    y_ssm = mixer(x_in, b_group, c_group, jnp.cumsum(log_decay, axis=0), step_size, skip)
    gated_pre = y_ssm * jax.nn.silu(gate_in.astype(jnp.float32))
    grouped = gated_pre.reshape(tok_rows, head_local // NORM_HEADS, NORM_HEADS * P_SIZE)
    mean_sq = jnp.mean(grouped * grouped, axis=2, keepdims=True)
    gated = (
        (grouped * lax.rsqrt(mean_sq + norm_eps)).reshape(tok_rows, chan_width) * norm_gain[None, :]
    ).astype(jnp.bfloat16)
    sign_value = jnp.where(walsh_sign == 1, 1.0, -1.0).astype(jnp.bfloat16)
    signed = gated * sign_value[None, :]
    partner = partner_2(signed, "sub", 0)
    own_float = signed.astype(jnp.float32)
    partner_float = partner.astype(jnp.float32)
    mixed = jnp.where(sub_index % 2 == 1, partner_float - own_float, own_float + partner_float)
    chan_index = lax.axis_index("chan")
    for bit_index in range(lax.axis_size("chan").bit_length() - 1):
        partner = partner_2(mixed.astype(jnp.bfloat16), "chan", bit_index).astype(mixed.dtype)
        chan_bit = chan_index // 2**bit_index % 2
        mixed = jnp.where(chan_bit == 1, partner - mixed, mixed + partner)
    scaled = rotate(mixed, power_two(channel_shift_power, 1), power_two(channel_shift_power, -1))
    return project(scaled, out_weight)


def solution(mesh):
    return jax.shard_map(
        body,
        mesh=mesh,
        in_specs=(
            P(("groups", "seq"), ("chan", "sub")),
            P(("groups", "seq"), "chan", None),
            P(("groups", "seq"), "chan", None),
            P(("groups", "seq"), ("chan", "sub")),
            P(("groups", "seq"), ("chan", "sub")),
            P(("chan", "sub")),
            P(("groups", "seq"), ("chan", "sub")),
            P(("chan", "sub")),
            P(("chan", "sub")),
            P(("chan", "sub")),
            P(("chan", "sub"), "seq"),
        ),
        out_specs=P(("groups", "seq", "chan", "sub"), None),
        check_vma=False,
    )
```

```python
import functools
import math

import jax
import jax.numpy as jnp
from jax import lax
from jax.experimental import pallas as pl
from jax.experimental.pallas import tpu as pltpu
from jax.sharding import PartitionSpec as P

LOCAL_HEADS = 128
P_SIZE = 64
G = 4
NORM_HEADS = 16


norm_eps = 1e-05
clip_level = 4.0
expo_levels = (-1, 0, 1, 2, 3)
lanes = 128
pieces = 4
MESH = pl.DeviceIdType.MESH


def partner_2(block, axis, bit):
    count = lax.axis_size(axis)
    route = []
    for low in range(count):
        high = low | 1 << bit
        if high != low and high < count:
            route += [(low, high), (high, low)]
    return lax.ppermute(block, axis, route)


def power_two(expo, sign_flip):
    result = jnp.zeros(expo.shape, jnp.float32)
    for level in expo_levels:
        result = result + jnp.where(
            expo == level, jnp.float32(2.0 ** (sign_flip * level)), jnp.float32(0.0)
        )
    return result


def sylvester(order):
    indices = jnp.arange(order, dtype=jnp.int32)
    oddness_flag = jnp.zeros((order, order), jnp.int32)
    for bit_index in range(order.bit_length() - 1):
        stride = 2**bit_index
        oddness_flag = oddness_flag + indices[:, None] // stride % 2 * (
            indices[None, :] // stride % 2
        )
    return (1 - 2 * (oddness_flag % 2)).astype(jnp.bfloat16)


def halves(value):
    upper = value.astype(jnp.bfloat16)
    return upper, (value - upper.astype(jnp.float32)).astype(jnp.bfloat16)


def dot32(left, right):
    return jnp.dot(left, right, preferred_element_type=jnp.float32)


def mixer_kernel(
    n,
    tile,
    x_ref,
    bt_ref,
    c_ref,
    cum_ref,
    step_ref,
    cumt_ref,
    stept_ref,
    skip_ref,
    y_ref,
    arrived,
    leaving,
    inner_ref,
    send,
    recv,
):
    me = lax.axis_index("seq")
    right, left = lax.rem(me + 1, n), lax.rem(me + n - 1, n)
    barrier = pltpu.get_barrier_semaphore()
    for near in (left, right):
        pl.semaphore_signal(barrier, inc=1, device_id={"seq": near}, device_id_type=MESH)

    rows, width = y_ref.shape
    tiles = width // tile
    cum = cum_ref[...]
    total = cum_ref[rows - 1 : rows, :]
    to_end = step_ref[...] * jnp.exp(total - cum)
    since = jnp.exp(cum)
    whole = jnp.exp(total)
    causal = lax.broadcasted_iota(jnp.int32, (rows, rows), 0) >= lax.broadcasted_iota(
        jnp.int32, (rows, rows), 1
    )
    inner_ref[...] = jnp.where(causal, dot32(c_ref[...], bt_ref[...]), 0.0)

    def pick(first, second):
        shape = (max(first.shape[0], second.shape[0]), lanes)
        low = lax.broadcasted_iota(jnp.int32, shape, 1) < P_SIZE
        return jnp.where(low, first, second)

    def spread(values, i):
        pairs = range(i * tile // P_SIZE, (i + 1) * tile // P_SIZE, lanes // P_SIZE)
        return jnp.concatenate(
            [pick(values[:, h : h + 1], values[:, h + 1 : h + 2]) for h in pairs], axis=1
        )

    def diagonal(h, block):
        differ = cum[:, h : h + 1] - cumt_ref[h : h + 1, :]
        mixing = jnp.exp(jnp.minimum(differ, 0.0)) * inner_ref[...] * stept_ref[h : h + 1, :]
        upper, lower = halves(mixing)
        return dot32(
            jnp.concatenate([upper, lower], axis=1), jnp.concatenate([block, block], axis=0)
        )

    def copy(i):
        return pltpu.make_async_remote_copy(
            src_ref=leaving.at[i],
            dst_ref=arrived.at[i],
            send_sem=send.at[i],
            recv_sem=recv.at[i],
            device_id={"seq": right},
            device_id_type=MESH,
        )

    pl.semaphore_wait(barrier, 2)

    for i in range(tiles):
        at = slice(i * tile, (i + 1) * tile)
        x_tile = x_ref[:, at].astype(jnp.float32)
        upper, lower = halves(x_tile * spread(to_end, i))
        own = dot32(bt_ref[...], upper) + dot32(bt_ref[...], lower)

        @pl.when(me == 0)
        def _():
            leaving[i] = own.astype(jnp.bfloat16)

        @pl.when(me > 0)
        def _():
            copy(i).wait_recv()
            leaving[i] = (arrived[i].astype(jnp.float32) * spread(whole, i) + own).astype(
                jnp.bfloat16
            )

        @pl.when(me + 1 < n)
        def _():
            copy(i).start()

        for k in range(i * tile, (i + 1) * tile, lanes):
            here = slice(k, k + lanes)
            block = x_ref[:, here]
            h = k // P_SIZE
            y_ref[:, here] = (
                pick(diagonal(h, block), diagonal(h + 1, block))
                + block.astype(jnp.float32) * skip_ref[:, here]
            )

        @pl.when(me > 0)
        def _():
            y_ref[:, at] += dot32(c_ref[...], arrived[i]) * spread(since, i)

    @pl.when(me + 1 < n)
    def _():
        for i in range(tiles):
            copy(i).wait_send()


def mixer(x_in, b_group, c_group, cumul, step_size, skip):
    n = lax.axis_size("seq")
    rows, width = x_in.shape
    tile = min(128, width)
    tiles = width // tile
    states = b_group.shape[1]
    vmem = pl.BlockSpec(memory_space=pltpu.VMEM)
    return pl.pallas_call(
        functools.partial(mixer_kernel, n, tile),
        out_shape=jax.ShapeDtypeStruct((rows, width), jnp.float32),
        in_specs=[vmem] * 8,
        out_specs=vmem,
        scratch_shapes=[
            pltpu.VMEM((tiles, states, tile), jnp.bfloat16),
            pltpu.VMEM((tiles, states, tile), jnp.bfloat16),
            pltpu.VMEM((rows, rows), jnp.float32),
            pltpu.SemaphoreType.DMA((tiles,)),
            pltpu.SemaphoreType.DMA((tiles,)),
        ],
        compiler_params=pltpu.CompilerParams(
            collective_id=0, has_side_effects=True, vmem_limit_bytes=48 * 2**20
        ),
    )(
        x_in,
        b_group.T,
        c_group,
        cumul,
        step_size,
        cumul.T,
        step_size.T,
        jnp.repeat(skip, P_SIZE)[None, :],
    )


def rotate_kernel(factor, mixed_ref, table_ref, up_ref, down_ref, out_ref):
    count = mixed_ref.shape[1] // lanes
    parts = [mixed_ref[:, i * lanes : (i + 1) * lanes] for i in range(count)]
    span = 1
    while span < count:
        for i in range(count):
            if not i & span:
                a, b = parts[i], parts[i + span]
                parts[i], parts[i + span] = a + b, a - b
        span *= 2
    table = table_ref[...]
    for i in range(count):
        at = slice(i * lanes, (i + 1) * lanes)
        upper, lower = halves(parts[i])
        rotated = (dot32(upper, table) + dot32(lower, table)) * factor
        quant = jnp.clip(rotated * up_ref[:, at], -clip_level, clip_level).astype(jnp.bfloat16)
        out_ref[:, at] = (quant.astype(jnp.float32) * down_ref[:, at]).astype(jnp.bfloat16)


def rotate(mixed, up, down):
    vmem = pl.BlockSpec(memory_space=pltpu.VMEM)
    return pl.pallas_call(
        functools.partial(rotate_kernel, 1.0 / math.sqrt(LOCAL_HEADS * P_SIZE)),
        out_shape=jax.ShapeDtypeStruct(mixed.shape, jnp.bfloat16),
        in_specs=[vmem] * 4,
        out_specs=vmem,
    )(mixed, sylvester(lanes), up[None, :], down[None, :])


def project_kernel(
    n,
    n_chan,
    n_sub,
    tile,
    scaled_ref,
    weight_hbm,
    out_ref,
    weight,
    slots,
    partial,
    slabs,
    summed,
    landed,
    local_sem,
    g_send,
    g_recv,
    s_send,
    s_recv,
    f_send,
    f_recv,
):
    me = lax.axis_index("seq")
    peers = n_chan * n_sub
    here = lax.axis_index("chan") * n_sub + lax.axis_index("sub")
    rows, feats = out_ref.shape[0], weight.shape[1]

    def slab_device(e):
        other = lax.rem(here + e, peers)
        return other, {"chan": other // n_sub, "sub": lax.rem(other, n_sub)}

    fetch = pltpu.make_async_copy(weight_hbm, weight, local_sem.at[0])
    own = pltpu.make_async_copy(scaled_ref, slots.at[me], local_sem.at[1])
    fetch.start()
    own.start()
    barrier = pltpu.get_barrier_semaphore()

    @pl.loop(1, n)
    def _(d):
        pl.semaphore_signal(
            barrier, inc=1, device_id={"seq": lax.rem(me + d, n)}, device_id_type=MESH
        )

    @pl.loop(1, peers)
    def _(e):
        pl.semaphore_signal(barrier, inc=1, device_id=slab_device(e)[1], device_id_type=MESH)

    pl.semaphore_wait(barrier, n - 1 + peers - 1)

    piece = slots.shape[1] // pieces

    def hop(k, q, way, source=None):
        return pltpu.make_async_remote_copy(
            src_ref=(slots.at[k] if source is None else source).at[pl.ds(q * piece, piece)],
            dst_ref=slots.at[k, pl.ds(q * piece, piece)],
            send_sem=g_send.at[way, k, q],
            recv_sem=g_recv.at[k, q],
            device_id={"seq": lax.rem(me + (1 if way == 1 else n - 1), n)},
            device_id_type=MESH,
        )

    def slab(k, e):
        other, device = slab_device(e)
        return pltpu.make_async_remote_copy(
            src_ref=partial.at[k, pl.ds(pl.multiple_of(other * rows, rows), rows)],
            dst_ref=slabs.at[k, e],
            send_sem=s_send.at[k, e],
            recv_sem=s_recv.at[k, e],
            device_id=device,
            device_id_type=MESH,
        )

    def finish(k, z):
        return pltpu.make_async_remote_copy(
            src_ref=summed.at[k],
            dst_ref=landed.at[me],
            send_sem=f_send.at[k],
            recv_sem=f_recv.at[z],
            device_id={"seq": k},
            device_id_type=MESH,
        )

    def when_valid(k, act):
        pl.when(jnp.logical_and(k >= 0, k < n))(lambda: act(k))

    def to_right(k, q, source=None):
        @pl.when(me + 1 < n)
        def _():
            hop(k, q, 1, source).start()

    def to_left(k, q, source=None):
        @pl.when(me > 0)
        def _():
            hop(k, q, 0, source).start()

    for q in range(pieces):
        to_right(me, q, scaled_ref)
        to_left(me, q, scaled_ref)
    own.wait()
    fetch.wait()

    def project_block(k):
        @pl.loop(0, feats // tile)
        def _(i):
            at = pl.ds(pl.multiple_of(i * tile, tile), tile)
            partial[k, :, at] = dot32(slots[k], weight[:, at]).astype(jnp.bfloat16)

        @pl.loop(1, peers)
        def _(e):
            slab(k, e).start()

    def reduce_block(k):
        @pl.loop(1, peers)
        def _(e):
            slab(k, e).wait_recv()

        mine = pl.ds(pl.multiple_of(here * rows, rows), rows)
        total = partial[k, mine, :].astype(jnp.float32)
        for e in range(1, peers):
            total = total + slabs[k, e].astype(jnp.float32)
        summed[k] = total.astype(jnp.bfloat16)

        @pl.when(k != me)
        def _():
            finish(k, me).start()

    project_block(me)

    @pl.loop(1, n)
    def _(j):
        for q in range(pieces):

            def from_left(k, q=q):
                hop(k, q, 1).wait_recv()
                to_right(k, q)

            def from_right(k, q=q):
                hop(k, q, 0).wait_recv()
                to_left(k, q)

            when_valid(me - j, from_left)
            when_valid(me + j, from_right)

        when_valid(me - j, project_block)
        when_valid(me + j, project_block)

        @pl.when(j == 1)
        def _():
            reduce_block(me)

        @pl.when(j > 1)
        def _():
            when_valid(me - j + 1, reduce_block)
            when_valid(me + j - 1, reduce_block)

    when_valid(me - n + 1, reduce_block)
    when_valid(me + n - 1, reduce_block)

    def columns(z):
        return pl.ds(pl.multiple_of(z * feats, feats), feats)

    out_ref[:, columns(me)] = summed[me]

    @pl.loop(1, n)
    def _(d):
        z = lax.rem(me + d, n)
        finish(z, z).wait_recv()
        out_ref[:, columns(z)] = landed[z]

    @pl.loop(1, n)
    def _(d):
        z = lax.rem(me + d, n)
        finish(z, z).wait_send()

    @pl.loop(0, n)
    def _(k):
        @pl.when(jnp.logical_and(k <= me, me + 1 < n))
        def _():
            for q in range(pieces):
                hop(k, q, 1).wait_send()

        @pl.when(jnp.logical_and(k >= me, me > 0))
        def _():
            for q in range(pieces):
                hop(k, q, 0).wait_send()

        @pl.loop(1, peers)
        def _(e):
            slab(k, e).wait_send()


def project(scaled, weight):
    n, n_chan, n_sub = (lax.axis_size(axis) for axis in ("seq", "chan", "sub"))
    peers = n_chan * n_sub
    rows, depth = scaled.shape
    feats = weight.shape[1]
    own_rows = rows // peers
    vmem = pl.BlockSpec(memory_space=pltpu.VMEM)
    dma = pltpu.SemaphoreType.DMA
    return pl.pallas_call(
        functools.partial(project_kernel, n, n_chan, n_sub, min(256, feats)),
        out_shape=jax.ShapeDtypeStruct((own_rows, n * feats), jnp.bfloat16),
        in_specs=[vmem, pl.BlockSpec(memory_space=pl.ANY)],
        out_specs=vmem,
        scratch_shapes=[
            pltpu.VMEM(weight.shape, jnp.bfloat16),
            pltpu.VMEM((n, rows, depth), jnp.bfloat16),
            pltpu.VMEM((n, rows, feats), jnp.bfloat16),
            pltpu.VMEM((n, peers, own_rows, feats), jnp.bfloat16),
            pltpu.VMEM((n, own_rows, feats), jnp.bfloat16),
            pltpu.VMEM((n, own_rows, feats), jnp.bfloat16),
            dma((2,)),
            dma((2, n, pieces)),
            dma((n, pieces)),
            dma((n, peers)),
            dma((n, peers)),
            dma((n,)),
            dma((n,)),
        ],
        compiler_params=pltpu.CompilerParams(
            collective_id=1, has_side_effects=True, vmem_limit_bytes=60 * 2**20
        ),
    )(scaled, weight)


def body(
    x_in,
    b_in,
    c_in,
    step_size,
    log_decay,
    skip,
    gate_in,
    norm_gain,
    walsh_sign,
    channel_shift_power,
    out_weight,
):
    tok_rows, chan_width = x_in.shape
    head_local = step_size.shape[1]
    head_group = LOCAL_HEADS // G
    sub_index = lax.axis_index("sub")
    group_local = sub_index * head_local // head_group
    b_group = lax.dynamic_slice_in_dim(b_in, group_local, 1, 1)[:, 0, :]
    c_group = lax.dynamic_slice_in_dim(c_in, group_local, 1, 1)[:, 0, :]
    y_ssm = mixer(x_in, b_group, c_group, jnp.cumsum(log_decay, axis=0), step_size, skip)
    gated_pre = y_ssm * jax.nn.silu(gate_in.astype(jnp.float32))
    grouped = gated_pre.reshape(tok_rows, head_local // NORM_HEADS, NORM_HEADS * P_SIZE)
    mean_sq = jnp.mean(grouped * grouped, axis=2, keepdims=True)
    gated = (
        (grouped * lax.rsqrt(mean_sq + norm_eps)).reshape(tok_rows, chan_width) * norm_gain[None, :]
    ).astype(jnp.bfloat16)
    sign_value = jnp.where(walsh_sign == 1, 1.0, -1.0).astype(jnp.bfloat16)
    signed = gated * sign_value[None, :]
    partner = partner_2(signed, "sub", 0)
    own_float = signed.astype(jnp.float32)
    partner_float = partner.astype(jnp.float32)
    mixed = jnp.where(sub_index % 2 == 1, partner_float - own_float, own_float + partner_float)
    chan_index = lax.axis_index("chan")
    for bit_index in range(lax.axis_size("chan").bit_length() - 1):
        partner = partner_2(mixed.astype(jnp.bfloat16), "chan", bit_index).astype(mixed.dtype)
        chan_bit = chan_index // 2**bit_index % 2
        mixed = jnp.where(chan_bit == 1, partner - mixed, mixed + partner)
    scaled = rotate(mixed, power_two(channel_shift_power, 1), power_two(channel_shift_power, -1))
    return project(scaled, out_weight)


def solution(mesh):
    return jax.shard_map(
        body,
        mesh=mesh,
        in_specs=(
            P(("groups", "seq"), ("chan", "sub")),
            P(("groups", "seq"), "chan", None),
            P(("groups", "seq"), "chan", None),
            P(("groups", "seq"), ("chan", "sub")),
            P(("groups", "seq"), ("chan", "sub")),
            P(("chan", "sub")),
            P(("groups", "seq"), ("chan", "sub")),
            P(("chan", "sub")),
            P(("chan", "sub")),
            P(("chan", "sub")),
            P(("chan", "sub"), "seq"),
        ),
        out_specs=P(("groups", "seq", "chan", "sub"), None),
        check_vma=False,
    )
```
